32 devices in a mesh: parts: 2 (over y), leaf: 4 (over z), vec: 2 (over x), sub: 2 (over core).
Axes of the slice: x: 2, y: 2, z: 4, core: 2. Of those that a mesh axis runs over, the one named last changes fastest.
Arguments:
- charges: float32 [64, 131072], P('vec', ('parts', 'leaf', 'sub')), parts along dimension 1, may hold values from -6 to 6
- coordinates: float32 [3, 131072], P(None, ('parts', 'leaf', 'sub')), parts along dimension 1, may hold values from 0 to 1, as said below
- near_lists: int32 [512, 8], P(('parts', 'leaf', 'sub')), parts along dimension 0, may hold values from -1 to 255, as said below
- far_lists: int32 [1008, 8], P(('parts', 'leaf', 'sub')), parts along dimension 0, may hold values from -1 to 503, as said below
- leaf_basis: float32 [512, 64, 256], P(('parts', 'leaf', 'sub')), parts along dimension 0, may hold values from -0.375 to 0.375
- local_transfer: float32 [496, 64, 128], P(('parts', 'leaf', 'sub')), parts along dimension 0, may hold values from -0.5 to 0.5
- skeleton: float32 [1008, 3, 64], P('parts'), parts along dimension 0, may hold values from 0 to 1
- top_transfer: float32 [12, 64, 128], P('parts'), parts along dimension 0, may hold values from -0.5 to 0.5
- top_skeleton: float32 [12, 3, 64], P('parts'), parts along dimension 0, may hold values from 0 to 1
Outputs:
- potentials: float32 [64, 131072], P('vec', ('parts', 'leaf', 'sub')), parts along dimension 1
The draws below stay inside these ranges and needn't reach their ends.
There are 2 independent parts, one for each index of `parts`. The reference program is written for one: setup_inputs(seed, part) draws one part's arguments, and reference() takes and returns one part's arrays. A program takes and returns all parts, laid end to end along the dimension named above; each array names one. Nothing has to cross between parts.
Inputs may be any that keep to these rules, and one draw needn't show every extreme that they name: `near_lists`: each leaf's list holds the leaf itself in slot 0 and in slot 1 the leaf 16 below it (above it where there is none); every entry lies within 16 leaves of its leaf; empty slots hold -1. `far_lists`: every entry names a cluster of the same level in the same subtree or in one of the two subtrees beside it; slot 0 is always filled and empty slots hold -1. `coordinates`: each leaf's points lie in a box of up to three Morton cells along each dimension that contains the leaf's own Morton cell.
All inputs are finite; a program needn't handle non-finite values.
Results may differ from the reference program's by a relative error of at most 0.0003.
Values sent between devices are 32-bit elements; how exact they have to be, the bound alone decides.
No kernel may reach another device: no remote copies, remote signals or barrier semaphores. Data moves between devices by JAX's collectives and lax.ppermute only.
A program may use at most 64 MiB of HBM per device.

```python
import jax
import jax.numpy as jnp
from jax import lax

LEAF_PTS = 256
RANK = 64
RHS = 64
NEAR_SLOTS = 8
FAR_SLOTS = 8
LEAF_DEV = 32
GROUPS = 8
LEAVES = 256
POINTS = 65536
NODE_DEV = 63
NEAR_REACH = 16


def draw_coordinates(key, part):
    leaf_ids = jnp.arange(LEAVES, dtype=jnp.int32)
    bit_count = LEAVES.bit_length() - 1
    cells = [jnp.zeros((LEAVES,), jnp.int32) for axis_pos in range(3)]
    extents = [1, 1, 1]
    for bit_pos in range(bit_count):
        axis_pos = bit_pos % 3
        digit = leaf_ids // 2 ** bit_pos % 2
        cells[axis_pos] = cells[axis_pos] + digit * extents[axis_pos]
        extents[axis_pos] = extents[axis_pos] * 2
    spread = jax.random.uniform(key, (3, LEAVES, LEAF_PTS), jnp.float32)
    columns = []
    for axis_pos in range(3):
        box_cells = min(3, extents[axis_pos])
        box_start = jnp.clip(cells[axis_pos] - 1, 0, extents[axis_pos] - box_cells)
        corner = box_start.astype(jnp.float32)[:, None]
        columns.append((corner + float(box_cells) * spread[axis_pos]) / float(extents[axis_pos]))
    return jnp.stack(columns, axis=0).reshape(3, POINTS).astype(jnp.float32)


def draw_near_lists(key, part):
    first_key, second_key = jax.random.split(jax.random.fold_in(key, 11))
    leaf_ids = jnp.arange(LEAVES, dtype=jnp.int32)
    mirror = jnp.where(leaf_ids >= NEAR_REACH, leaf_ids - NEAR_REACH, leaf_ids + NEAR_REACH)
    offsets = jax.random.randint(first_key, (LEAVES, NEAR_SLOTS - 2), -NEAR_REACH, NEAR_REACH + 1)
    others = leaf_ids[:, None] + offsets
    chance = jax.random.randint(second_key, (LEAVES, NEAR_SLOTS - 2), 0, 4)
    keep = jnp.logical_and(jnp.logical_and(others >= 0, others < LEAVES), chance > 0)
    others = jnp.where(keep, others, -1)
    return jnp.concatenate([leaf_ids[:, None], mirror[:, None], others], axis=1).astype(jnp.int32)


def draw_far_lists(key, part):
    first_key, second_key, third_key = jax.random.split(jax.random.fold_in(key, 23), 3)
    nodes = GROUPS * NODE_DEV
    node_ids = jnp.arange(nodes, dtype=jnp.int32)
    owner = node_ids // NODE_DEV
    slot = node_ids % NODE_DEV
    level_count = jnp.ones((nodes,), jnp.int32)
    level_first = jnp.zeros((nodes,), jnp.int32)
    count = LEAF_DEV
    start = 0
    while count >= 1:
        inside = jnp.logical_and(slot >= start, slot < start + count)
        level_count = jnp.where(inside, count, level_count)
        level_first = jnp.where(inside, start, level_first)
        start = start + count
        count = count // 2
    shift = jax.random.randint(first_key, (nodes, FAR_SLOTS), -1, 2)
    partner_owner = jnp.clip(owner[:, None] + shift, 0, GROUPS - 1)
    within = jax.random.randint(second_key, (nodes, FAR_SLOTS), 0, 1 << 20) % level_count[:, None]
    entry = partner_owner * NODE_DEV + level_first[:, None] + within
    filled = jax.random.randint(third_key, (nodes, 1), 1, FAR_SLOTS + 1)
    filled = filled.at[0, 0].set(FAR_SLOTS)
    keep = jnp.arange(FAR_SLOTS, dtype=jnp.int32)[None, :] < filled
    return jnp.where(keep, entry, -1).astype(jnp.int32)


def shard_levels(own_key, dims, cuts, smallest, high):
    loudness = 1.0
    for axis_at, parts in cuts:
        draws = jax.random.uniform(jax.random.fold_in(jax.random.fold_in(own_key, 6), axis_at), (parts,), jnp.float32, smallest / len(cuts), high / len(cuts))
        loudness = loudness * jnp.repeat(jnp.exp(draws), dims[axis_at] // parts).reshape((-1,) + (1,) * (len(dims) - 1 - axis_at))
    return loudness


def scatter_about(own_key, shape, width, limit, cuts=(), kind=jnp.bfloat16):
    entries = jax.random.normal(own_key, shape, jnp.float32) * width
    if len(cuts) > 0:
        entries = shard_levels(own_key, shape, cuts, -0.22, 0.18) * entries
    return jnp.clip(entries, min=-limit, max=limit).astype(kind)


def setup_inputs(seed: int = 0, part: int = 0) -> dict:
    key_list = jax.random.split(jax.random.key(seed), 10)
    part_keys = jax.random.split(jax.random.fold_in(key_list[9], part), 10)
    return {
        "charges": scatter_about(part_keys[0], (RHS, POINTS), 1.0, 6.0, ((0, 2), (1, 8)), jnp.float32),
        "coordinates": draw_coordinates(jax.random.fold_in(jax.random.fold_in(key_list[9], part), 71), part),
        "near_lists": draw_near_lists(jax.random.fold_in(jax.random.fold_in(key_list[9], part), 71), part),
        "far_lists": draw_far_lists(jax.random.fold_in(jax.random.fold_in(key_list[9], part), 71), part),
        "leaf_basis": scatter_about(part_keys[4], (LEAVES, RANK, LEAF_PTS), LEAF_PTS ** -0.5, 0.375, ((0, 8),), jnp.float32),
        "local_transfer": scatter_about(part_keys[5], (GROUPS * (LEAF_DEV - 1), RANK, 2 * RANK), (2 * RANK) ** -0.5, 0.5, ((0, 8),), jnp.float32),
        "skeleton": jnp.clip(jax.random.uniform(part_keys[6], (GROUPS * NODE_DEV, 3, RANK), jnp.float32, 0.0, 1.0), 0.0, 1.0),
        "top_transfer": scatter_about(part_keys[7], (GROUPS - 2, RANK, 2 * RANK), (2 * RANK) ** -0.5, 0.5, (), jnp.float32),
        "top_skeleton": jnp.clip(jax.random.uniform(part_keys[8], (GROUPS - 2, 3, RANK), jnp.float32, 0.0, 1.0), 0.0, 1.0),
    }


KERNEL_WIDTH = 0.05
NEAR_WEIGHT = 0.0625
exact_mode = lax.Precision.HIGHEST

def kernel_block(targets, sources):
    total = None
    for axis_pos in range(3):
        differ = targets[..., axis_pos, :, None] - sources[..., axis_pos, None, :]
        total = differ * differ if total is None else total + differ * differ
    return KERNEL_WIDTH / jnp.sqrt(total + KERNEL_WIDTH * KERNEL_WIDTH)

def reference(charges, coordinates, near_lists, far_lists, leaf_basis, local_transfer, skeleton, top_transfer, top_skeleton):
    groups = GROUPS
    leaf_charges = charges.reshape(RHS, LEAVES, LEAF_PTS).transpose(1, 0, 2)
    leaf_points = coordinates.reshape(3, LEAVES, LEAF_PTS).transpose(1, 0, 2)

    def near_block(start):
        rows = lax.dynamic_slice_in_dim(near_lists, start, 4, 0)
        valid = (rows >= 0).astype(jnp.float32)
        picked = jnp.clip(rows, 0, LEAVES - 1)
        targets = lax.dynamic_slice_in_dim(leaf_points, start, 4, 0)
        source_points = leaf_points[picked]
        source_charges = leaf_charges[picked] * valid[:, :, None, None]
        tiles = kernel_block(targets[:, None], source_points)
        return jnp.einsum('betd,bevd->bvt', tiles, source_charges, precision=exact_mode)
    block_starts = (jnp.arange(LEAVES // 4) * 4).astype(jnp.int32)
    near = lax.map(near_block, block_starts).reshape(LEAVES, RHS, LEAF_PTS)
    leaf_coef = jnp.einsum('kvd,krd->kvr', leaf_charges, leaf_basis, precision=exact_mode)
    transfers = local_transfer.reshape(groups, LEAF_DEV - 1, RANK, 2 * RANK)
    current = leaf_coef.reshape(groups, LEAF_DEV, RHS, RANK)
    level_coefs = [current]
    level_sizes = [LEAF_DEV]
    level_starts = [0]
    count = LEAF_DEV
    slot_start = 0
    while count > 1:
        half = count // 2
        slot_start = slot_start + count
        paired = current.reshape(groups, half, 2, RHS, RANK).transpose(0, 1, 3, 2, 4).reshape(groups, half, RHS, 2 * RANK)
        mats = transfers[:, slot_start - LEAF_DEV:slot_start - LEAF_DEV + half]
        current = jnp.einsum('ghva,ghra->ghvr', paired, mats, precision=exact_mode)
        level_coefs.append(current)
        level_sizes.append(half)
        level_starts.append(slot_start)
        count = half
    node_coef = jnp.concatenate(level_coefs, axis=1)
    flat_coef = node_coef.reshape(groups * NODE_DEV, RHS, RANK)
    skel_groups = skeleton.reshape(groups, NODE_DEV, 3, RANK)
    lists = far_lists.reshape(groups, NODE_DEV, FAR_SLOTS)

    def far_group(inputs):
        group_lists, group_skel = inputs
        valid = (group_lists >= 0).astype(jnp.float32)
        picked = jnp.clip(group_lists, 0, groups * NODE_DEV - 1)
        source_skel = skeleton[picked]
        source_coef = flat_coef[picked] * valid[:, :, None, None]
        tiles = kernel_block(group_skel[:, None], source_skel)
        return jnp.einsum('nerj,nevj->nvr', tiles, source_coef, precision=exact_mode)
    far = lax.map(far_group, (lists, skel_groups))
    top_bits = groups.bit_length() - 1
    current = node_coef[:, NODE_DEV - 1]
    couplings = []
    for height in range(top_bits):
        count = groups >> height
        if height == 0:
            skel_now = skel_groups[:, NODE_DEV - 1]
        else:
            start = groups - (groups >> height - 1)
            skel_now = top_skeleton[start:start + count]
        pair_skel = skel_now.reshape(count // 2, 2, 3, RANK)[:, ::-1].reshape(count, 3, RANK)
        pair_coef = current.reshape(count // 2, 2, RHS, RANK)[:, ::-1].reshape(count, RHS, RANK)
        tiles = kernel_block(skel_now, pair_skel)
        couplings.append(jnp.einsum('nrj,nvj->nvr', tiles, pair_coef, precision=exact_mode))
        if height < top_bits - 1:
            start = groups - (groups >> height)
            mats = top_transfer[start:start + count // 2]
            paired = current.reshape(count // 2, 2, RHS, RANK).transpose(0, 2, 1, 3).reshape(count // 2, RHS, 2 * RANK)
            current = jnp.einsum('nva,nra->nvr', paired, mats, precision=exact_mode)
    top_local = couplings[top_bits - 1]
    for height in range(top_bits - 2, -1, -1):
        count = groups >> height
        start = groups - (groups >> height)
        mats = top_transfer[start:start + count // 2]
        spread = jnp.einsum('nvr,nra->nva', top_local, mats, precision=exact_mode)
        spread = spread.reshape(count // 2, RHS, 2, RANK).transpose(0, 2, 1, 3).reshape(count, RHS, RANK)
        top_local = couplings[height] + spread
    level_locals = [far[:, level_starts[pos]:level_starts[pos] + level_sizes[pos]] for pos in range(len(level_sizes))]
    level_locals[-1] = level_locals[-1] + top_local[:, None]
    for pos in range(len(level_sizes) - 2, -1, -1):
        parent = level_locals[pos + 1]
        parent_count = level_sizes[pos + 1]
        first = level_starts[pos + 1] - LEAF_DEV
        mats = transfers[:, first:first + parent_count]
        spread = jnp.einsum('ghvr,ghra->ghva', parent, mats, precision=exact_mode)
        spread = spread.reshape(groups, parent_count, RHS, 2, RANK).transpose(0, 1, 3, 2, 4).reshape(groups, 2 * parent_count, RHS, RANK)
        level_locals[pos] = level_locals[pos] + spread
    leaf_local = level_locals[0].reshape(LEAVES, RHS, RANK)
    far_part = jnp.einsum('kvr,krd->kvd', leaf_local, leaf_basis, precision=exact_mode)
    total = far_part + NEAR_WEIGHT * near
    return total.transpose(1, 0, 2).reshape(RHS, POINTS)
```

```python
import functools

import jax
import jax.numpy as jnp
import numpy as np
from jax import lax
from jax.experimental import pallas as pl
from jax.experimental.pallas import tpu as pltpu
from jax.sharding import PartitionSpec as P

PTS = 256
RANK = 64
LEAVES = 32
NODES = 63
SLOTS = 8
REACH = 16
HALF = REACH * PTS
ROWS = 8
PAD = 16
GROUP = 4
WIDTH = 0.05
NEAR_WEIGHT = 0.0625
EMPTY = 3 * 64
F32 = jnp.float32
BF16 = jnp.bfloat16
AXES = ("leaf", "sub")
NN = (((1,), (0,)), ((), ()))
NT = (((1,), (1,)), ((), ()))
TN = (((0,), (0,)), ((), ()))


def selections():
    source_part = (1, 1, 2, 2, 1, 3)
    target_part = (1, 2, 1, 2, 3, 1)
    source = np.zeros((64, 32), np.float32)
    target = np.zeros((32, 64), np.float32)
    for g in range(6):
        for c in range(3):
            source[(source_part[g] - 1) * 8 + c, 4 * g + c] = 1
            target[4 * g + c, (target_part[g] - 1) * 8 + c] = -2
        f = 4 * g + 3
        if g < 3:
            source[24 + 8 * g, f] = 1
            target[f, 48] = 1
        else:
            source[48, f] = 1
            target[f, 24 + 8 * (g - 3)] = 1
    source[48, 24] = 1
    target[24, 48] = 1
    wide = np.zeros((64, 256), np.float32)
    wide[:, :32] = source
    wide[:, 128 + 32 : 128 + 64] = source
    return jnp.asarray(wide, BF16), jnp.asarray(target, BF16)


def halves(x):
    high = x.astype(BF16)
    return high, (x - high.astype(F32)).astype(BF16)


def dot(a, b, dims=NN):
    return lax.dot_general(a, b, dims, preferred_element_type=F32)


def dot3(a, b, dims=NN):
    ah, al = halves(a)
    bh, bl = halves(b)
    rows = a.shape[0]
    both = dot(jnp.concatenate([ah, al], axis=0), bh, dims)
    return both[:rows] + both[rows:] + dot(ah, bl, dims)


def parts_of(points):
    n = points.shape[1]
    c = (points - 0.5) * (1.0 / WIDTH)
    c = jnp.concatenate([c, jnp.zeros((5, n), F32)], axis=0)

    def rounded(x):
        return x.astype(BF16).astype(F32)

    p1 = rounded(c)
    rest = c - p1
    p2 = rounded(rest)
    p3 = rest - p2
    norm = jnp.broadcast_to(jnp.sum(c * c, axis=0, keepdims=True), (8, n))
    n1 = rounded(norm)
    rest = norm - n1
    n2 = rounded(rest)
    n3 = rest - n2
    rows = [p1, p2, p3, n1, n2, n3, jnp.ones((8, n), F32), jnp.zeros((8, n), F32)]
    return jnp.concatenate(rows, axis=0).astype(BF16)


def lower_lanes(rows):
    return lax.broadcasted_iota(jnp.int32, (rows, 128), 1) < RANK


def diagonal(x, vectors):
    return jnp.where(lower_lanes(vectors), x[:vectors], x[vectors:])


def spread_pair(pair):
    low = lower_lanes(pair.shape[0])
    zero = jnp.zeros_like(pair)
    return jnp.concatenate([jnp.where(low, pair, zero), jnp.where(low, zero, pair)], axis=0)


def pipelined(steps, first, second):
    for u in range(GROUP):
        first(u, u, 0)

    def body(i, carry):
        for h in range(2):
            base = (2 * i + h) * GROUP
            for u in range(GROUP):
                first(base + GROUP + u, u, 1 - h)
            for u in range(GROUP):
                second(base + u, u, h)
        return carry

    lax.fori_loop(0, (steps + 2 * GROUP - 1) // (2 * GROUP), body, 0)


def up_kernel(
    near_ref, far_ref, far_vec, charges_hbm, coords_hbm, basis_hbm, transfer_hbm,
    up_ref, down_ref, root_ref, local_ref, halo_ref, steps_ref, count_ref, entry_ref,
    charges, coords, basis, transfer, coef, sems,
):
    vectors = charges.shape[0]
    copies = [
        pltpu.make_async_copy(charges_hbm, charges, sems.at[0]),
        pltpu.make_async_copy(basis_hbm, basis, sems.at[1]),
        pltpu.make_async_copy(transfer_hbm, transfer, sems.at[2]),
        pltpu.make_async_copy(coords_hbm, coords, sems.at[3]),
    ]
    for copy in copies:
        copy.start()
    device = lax.axis_index(AXES)
    first = device * LEAVES

    def scan_leaf(t, counts):
        here, there = counts
        for e in range(SLOTS):
            entry = near_ref[t, e]
            s = entry - first
            inside = jnp.logical_and(s >= 0, s < LEAVES)
            outside = jnp.logical_and(entry >= 0, jnp.logical_not(inside))
            local_ref[here] = t * 256 + s
            halo_ref[there] = t * 256 + jnp.where(s < 0, s + REACH, s - REACH)
            here = here + inside.astype(jnp.int32)
            there = there + outside.astype(jnp.int32)
        return here, there

    here, there = lax.fori_loop(0, LEAVES, scan_leaf, (jnp.int32(0), jnp.int32(0)))
    for u in range(PAD):
        local_ref[here + u] = LEAVES
        halo_ref[there + u] = LEAVES
    for p in range(32):
        steps_ref[p] = p * 256 + 2 * p

    def scan_pair(p, count):
        top = far_ref[2 * p, 4]
        for e in range(4):
            for c in range(2):
                top = jnp.maximum(top, far_ref[jnp.minimum(2 * p + c, NODES - 1), 4 + e])
        steps_ref[count] = p * 256 + 2 * p + 1
        return count + (top >= 0).astype(jnp.int32)

    total = lax.fori_loop(0, 32, scan_pair, jnp.int32(32))
    for u in range(PAD):
        steps_ref[total + u] = 32 * 256
    count_ref[0] = here
    count_ref[1] = there
    count_ref[2] = total
    entry = far_vec[...]
    place = entry - (device - 1) * NODES
    place = place + (place >= NODES).astype(jnp.int32) + (place >= 2 * NODES).astype(jnp.int32)
    place = jnp.where(entry >= 0, place, EMPTY)
    entry_ref[0:NODES] = place
    entry_ref[NODES:64] = jnp.full((1, SLOTS), EMPTY, jnp.int32)

    copies[0].wait()
    copies[1].wait()

    def put(pair, value):
        coef[pair] = value

    for p in range(LEAVES // 2):
        a, b = slice(2 * p * PTS, (2 * p + 1) * PTS), slice((2 * p + 1) * PTS, (2 * p + 2) * PTS)
        both = jnp.concatenate([charges[:, a], charges[:, b]], axis=0)
        put(p, diagonal(dot3(both, basis[2 * p : 2 * p + 2].reshape(2 * RANK, PTS), NT), vectors))
    copies[2].wait()
    for p in range(LEAVES // 2, LEAVES - 1):
        q = 2 * p - LEAVES
        both = coef[q : q + 2].reshape(2 * vectors, 128)
        put(p, diagonal(dot3(both, transfer[q : q + 2].reshape(128, 128), NT), vectors))
    root = dot3(coef[30], transfer[30], NT)
    root = jnp.concatenate([root, jnp.zeros((vectors, RANK), F32)], axis=1)
    put(31, root)
    root_ref[...] = root
    copies[3].wait()
    up_ref[0:vectors] = charges[:, HALF:]
    down_ref[0:vectors] = charges[:, :HALF]
    for p in range(LEAVES):
        lanes = slice(p * 128, (p + 1) * 128)
        up_ref[vectors : 2 * vectors, lanes] = coef[p]
        down_ref[vectors : 2 * vectors, lanes] = coef[p]
    up_ref[2 * vectors : 2 * vectors + 3] = coords[:, HALF:]
    down_ref[2 * vectors : 2 * vectors + 3] = coords[:, :HALF]
    up_ref[2 * vectors + 3 :] = jnp.zeros((5, HALF), F32)
    down_ref[2 * vectors + 3 :] = jnp.zeros((5, HALF), F32)


def source_tables(k, charges, points, select, sources, weights):
    parts = parts_of(points)
    sources[k] = dot(parts, select[:, 0:32], TN).astype(BF16)
    high, low = halves(charges)
    weights[k] = jnp.concatenate([high, low], axis=0)
    return parts


def near_steps(list_ref, sources, targets, weights, out_ref, tiles):
    vectors = out_ref.shape[0]
    highs = (tiles[:GROUP], tiles[GROUP : 2 * GROUP])
    lows = (tiles[2 * GROUP : 3 * GROUP], tiles[3 * GROUP :])

    def decode(j):
        code = list_ref[j]
        return lax.shift_right_logical(code, 8), jnp.bitwise_and(code, 255)

    def first(j, u, b):
        t, s = decode(j)
        high, low = halves(lax.rsqrt(dot(sources[s], targets[t])))
        highs[b][u][...] = high
        lows[b][u][...] = low

    def second(j, u, b):
        t, s = decode(j)
        q = weights[s]
        both = dot(q, highs[b][u][...])
        lanes = pl.ds(pl.multiple_of(t * PTS, PTS), PTS)
        out_ref[:, lanes] += both[:vectors] + both[vectors:] + dot(q[:vectors], lows[b][u][...])

    return first, second


def near_kernel(
    count_ref, list_ref, charges, coords, select, select_t,
    near_ref, targets_ref, sources, weights, *tiles,
):
    vectors = charges.shape[0]
    for k in range(LEAVES):
        lanes = slice(k * PTS, (k + 1) * PTS)
        parts = source_tables(k, charges[:, lanes], coords[:, lanes], select, sources, weights)
        targets_ref[k] = dot(select_t[...], parts).astype(BF16)
    weights[LEAVES] = jnp.zeros((2 * vectors, PTS), BF16)
    sources[LEAVES] = sources[0]
    near_ref[...] = jnp.zeros_like(near_ref)
    first, second = near_steps(list_ref, sources, targets_ref, weights, near_ref, tiles)
    pipelined(count_ref[0], first, second)


def down_kernel(
    groups, count_ref, list_ref, steps_ref, entry_ref,
    near, targets, lower, own, upper, roots, basis, transfer,
    skel0, skel1, skel2, top_transfer, top_skeleton, select, select_t,
    out_ref,
    sources, weights, skel_points, skel_even, skel_odd, skel_targets,
    coef_low, coef_high, local, top_coef, *tiles,
):
    vectors = near.shape[0]
    device = lax.axis_index(AXES)
    low_mask = lower_lanes(vectors)
    for k in range(LEAVES):
        buffer = lower if k < REACH else upper
        lanes = slice((k % REACH) * PTS, (k % REACH + 1) * PTS)
        source_tables(
            k, buffer[0:vectors, lanes], buffer[2 * vectors : 2 * vectors + 3, lanes],
            select, sources, weights,
        )
    weights[LEAVES] = jnp.zeros((2 * vectors, PTS), BF16)
    sources[LEAVES] = sources[0]
    out_ref[...] = near[...]
    first, second = near_steps(list_ref, sources, targets, weights, out_ref, tiles)
    pipelined(count_ref[1], first, second)

    for b, skel in enumerate((skel0, skel1, skel2)):
        for p in range(32):
            left = skel[2 * p]
            right = skel[2 * p + 1] if p < 31 else jnp.zeros((3, RANK), F32)
            skel_points[b, :, p * 128 : (p + 1) * 128] = jnp.concatenate([left, right], axis=1)
        for g in range(8):
            lanes = slice(g * 512, (g + 1) * 512)
            parts = parts_of(skel_points[b, :, lanes])
            feature = dot(parts, select[...], TN).astype(BF16).reshape(8, RANK, 256)
            skel_even[b * 64 + g * 8 : b * 64 + (g + 1) * 8] = feature[:, :, 0:RANK]
            skel_odd[b * 64 + g * 8 : b * 64 + (g + 1) * 8] = feature[:, :, 128 : 128 + RANK]
            if b == 1:
                target = dot(select_t[...], parts)
                for u in range(4):
                    skel_targets[g * 4 + u] = spread_pair(target[:, u * 128 : (u + 1) * 128]).astype(BF16)
    skel_even[EMPTY] = skel_even[0]
    skel_odd[EMPTY] = skel_odd[0]
    for b, buffer in enumerate((lower, own, upper)):
        for p in range(32):
            pair = buffer[vectors : 2 * vectors, p * 128 : (p + 1) * 128]
            swap = pltpu.roll(pair, RANK, 1)
            zero = jnp.zeros_like(pair)
            for n, (a, c) in enumerate(((pair, swap), (swap, pair))):
                for table, value in (
                    (coef_low, jnp.where(low_mask, a, zero)),
                    (coef_high, jnp.where(low_mask, zero, c)),
                ):
                    high, low = halves(value)
                    table[b * 64 + 2 * p + n] = jnp.concatenate([high, low], axis=0)
    coef_low[EMPTY] = jnp.zeros((2 * vectors, 128), BF16)
    coef_high[EMPTY] = jnp.zeros((2 * vectors, 128), BF16)
    local[...] = jnp.zeros_like(local)

    far_highs = (tiles[:GROUP], tiles[GROUP : 2 * GROUP])
    far_lows = (tiles[2 * GROUP : 3 * GROUP], tiles[3 * GROUP :])

    def entries(j):
        code = steps_ref[j]
        target = lax.shift_right_logical(code, 8)
        chunk = jnp.bitwise_and(code, 255)
        p = lax.shift_right_logical(chunk, 1)
        slot = 4 * jnp.bitwise_and(chunk, 1)
        even = [entry_ref[2 * p, slot + e] for e in range(4)]
        odd = [entry_ref[2 * p + 1, slot + e] for e in range(4)]
        return target, p, even, odd

    def far_first(j, u, b):
        target, p, even, odd = entries(j)
        rows = [skel_even[even[e]] + skel_odd[odd[e]] for e in range(4)]
        x = dot(jnp.concatenate(rows, axis=0), skel_targets[p])
        high, low = halves(lax.rsqrt(x))
        far_highs[b][u][:, 0:128] = high
        far_lows[b][u][:, 0:128] = low

    def far_second(j, u, b):
        target, p, even, odd = entries(j)

        def side(s):
            return jnp.concatenate(
                [coef_low[s[0]] + coef_high[s[1]], coef_low[s[2]] + coef_high[s[3]]], axis=1
            )

        sides = (side(even), side(odd))
        empty = jnp.logical_or(target == 32, False)
        stack = jnp.concatenate(
            [sides[0][:vectors], sides[1][:vectors], sides[0][vectors:], sides[1][vectors:]], axis=0
        )
        both = dot(stack, far_highs[b][u][:, 0:128])
        total = both[: 2 * vectors] + both[2 * vectors :]
        total = total + dot(stack[: 2 * vectors], far_lows[b][u][:, 0:128])
        local[target] += diagonal(total, vectors)

    pipelined(count_ref[2], far_first, far_second)

    bits = groups.bit_length() - 1
    offsets = []
    offset = 0
    for h in range(bits):
        count = groups >> h
        offsets.append(offset)
        for i in range(count // 2):
            if h == 0:
                pair = roots[2 * i] + pltpu.roll(roots[2 * i + 1], RANK, 1)
            else:
                start = groups - (groups >> (h - 1)) + 2 * i
                below = offsets[h - 1] + 2 * i
                both = top_coef[below : below + 2].reshape(2 * vectors, 128)
                matrix = top_transfer[start : start + 2].reshape(128, 128)
                pair = diagonal(dot3(both, matrix, NT), vectors)
            top_coef[offset + i] = pair
        offset += count // 2
    row = lax.broadcasted_iota(jnp.int32, (128, 128), 0) < RANK
    lane = lax.broadcasted_iota(jnp.int32, (128, 128), 1) < RANK
    couple = []
    for h in range(bits):
        node = device // 2**h
        i = node // 2
        if h == 0:
            odd = node % 2 == 1
            left = jnp.where(odd, skel0[NODES - 1], skel1[NODES - 1])
            right = jnp.where(odd, skel1[NODES - 1], skel2[NODES - 1])
        else:
            start = groups - (groups >> (h - 1))
            left = top_skeleton[start + 2 * i]
            right = top_skeleton[start + 2 * i + 1]
        parts = parts_of(jnp.concatenate([left, right], axis=1))
        feature = dot(parts, select[:, 0:32], TN).astype(BF16)
        target = dot(select_t[...], parts).astype(BF16)
        tile = jnp.where(row != lane, lax.rsqrt(dot(feature, target)), 0.0)
        couple.append(dot3(top_coef[offsets[h] + i], tile))
    top = couple[bits - 1]
    for h in range(bits - 2, -1, -1):
        parent = device // 2 ** (h + 1)
        mine = jnp.where(low_mask == (parent % 2 == 0), top, 0.0)
        start = groups - (groups >> h) + 2 * (parent // 2)
        matrix = top_transfer[pl.ds(start, 2)].reshape(128, 128)
        top = couple[h] + dot3(mine, matrix)
    top = jnp.where(device % 2 == 1, pltpu.roll(top, RANK, 1), top)

    local[30] += dot3(jnp.where(low_mask, local[31] + top, 0.0)[:, :RANK], transfer[30])
    for p in range(30, 15, -1):
        q = 2 * p - LEAVES
        both = dot3(spread_pair(local[p]), transfer[q : q + 2].reshape(128, 128))
        local[q] += both[:vectors]
        local[q + 1] += both[vectors:]
    for p in range(LEAVES // 2):
        both = dot3(spread_pair(local[p]), basis[2 * p : 2 * p + 2].reshape(128, PTS))
        for c in range(2):
            lanes = slice((2 * p + c) * PTS, (2 * p + c + 1) * PTS)
            out_ref[:, lanes] = both[c * vectors : (c + 1) * vectors] + NEAR_WEIGHT * out_ref[:, lanes]


def whole(count, space=pltpu.VMEM):
    return [pl.BlockSpec(memory_space=space)] * count


def on_device(
    charges, coordinates, near_lists, far_lists, leaf_basis, local_transfer,
    skeleton, top_transfer, top_skeleton,
):
    vectors = charges.shape[0]
    groups = lax.axis_size(AXES)
    points = LEAVES * PTS
    height = 2 * vectors + ROWS
    shape = jax.ShapeDtypeStruct
    select, select_t = selections()
    params = pltpu.CompilerParams(vmem_limit_bytes=56 << 20)
    smem = pltpu.SMEM
    up, down, root, local_list, halo_list, steps, counts, entries = pl.pallas_call(
        up_kernel,
        out_shape=[
            shape((height, HALF), F32),
            shape((height, HALF), F32),
            shape((vectors, 128), F32),
            shape((LEAVES * SLOTS + PAD,), jnp.int32),
            shape((LEAVES * SLOTS + PAD,), jnp.int32),
            shape((64 + PAD,), jnp.int32),
            shape((3,), jnp.int32),
            shape((64, SLOTS), jnp.int32),
        ],
        in_specs=whole(2, smem) + whole(1) + whole(4, pl.ANY),
        out_specs=whole(3) + whole(4, smem) + whole(1),
        scratch_shapes=[
            pltpu.VMEM((vectors, points), F32),
            pltpu.VMEM((3, points), F32),
            pltpu.VMEM((LEAVES, RANK, PTS), F32),
            pltpu.VMEM((LEAVES - 1, RANK, 128), F32),
            pltpu.VMEM((LEAVES, vectors, 128), F32),
            pltpu.SemaphoreType.DMA((4,)),
        ],
        compiler_params=params,
    )(near_lists, far_lists, far_lists, charges, coordinates, leaf_basis, local_transfer)

    upward = [(i, i + 1) for i in range(groups - 1)]
    lower = lax.ppermute(up, AXES, upward)
    upper = lax.ppermute(down, AXES, [(j, i) for i, j in upward])
    roots = lax.all_gather(root, AXES)

    tiles = [pltpu.VMEM((PTS, PTS), BF16)] * (4 * GROUP)
    near, targets = pl.pallas_call(
        near_kernel,
        out_shape=[shape((vectors, points), F32), shape((LEAVES, 32, PTS), BF16)],
        in_specs=whole(2, smem) + whole(4),
        out_specs=whole(2),
        scratch_shapes=[
            pltpu.VMEM((LEAVES + 1, PTS, 32), BF16),
            pltpu.VMEM((LEAVES + 1, 2 * vectors, PTS), BF16),
        ]
        + tiles,
        compiler_params=params,
        cost_estimate=pl.CostEstimate(
            flops=192 * 3 * 2 * PTS**3, transcendentals=192 * PTS**2, bytes_accessed=4 << 20
        ),
    )(counts, local_list, charges, coordinates, select, select_t)

    def block(shift):
        def index(i):
            device = lax.axis_index(AXES)
            return (jnp.clip(device + shift, 0, groups - 1), 0, 0)

        return pl.BlockSpec((NODES, 3, RANK), index)

    return pl.pallas_call(
        functools.partial(down_kernel, groups),
        out_shape=shape((vectors, points), F32),
        grid=(1,),
        in_specs=whole(4, smem)
        + whole(8)
        + [block(-1), block(0), block(1)]
        + whole(4),
        out_specs=pl.BlockSpec(memory_space=pltpu.VMEM),
        scratch_shapes=[
            pltpu.VMEM((LEAVES + 1, PTS, 32), BF16),
            pltpu.VMEM((LEAVES + 1, 2 * vectors, PTS), BF16),
            pltpu.VMEM((3, 3, HALF), F32),
            pltpu.VMEM((EMPTY + 1, RANK, RANK), BF16),
            pltpu.VMEM((EMPTY + 1, RANK, RANK), BF16),
            pltpu.VMEM((32, RANK, 128), BF16),
            pltpu.VMEM((EMPTY + 1, 2 * vectors, 128), BF16),
            pltpu.VMEM((EMPTY + 1, 2 * vectors, 128), BF16),
            pltpu.VMEM((33, vectors, 128), F32),
            pltpu.VMEM((groups, vectors, 128), F32),
        ]
        + tiles,
        compiler_params=params,
    )(
        counts, halo_list, steps, entries, near, targets, lower, up, upper, roots,
        leaf_basis, local_transfer, skeleton, skeleton, skeleton, top_transfer, top_skeleton,
        select, select_t,
    )


def solution(mesh):
    placed = (
        P("vec", ("parts", "leaf", "sub")),
        P(None, ("parts", "leaf", "sub")),
        P(("parts", "leaf", "sub"), None),
        P(("parts", "leaf", "sub"), None),
        P(("parts", "leaf", "sub"), None, None),
        P(("parts", "leaf", "sub"), None, None),
        P("parts", None, None),
        P("parts", None, None),
        P("parts", None, None),
    )
    return jax.shard_map(
        on_device,
        mesh=mesh,
        in_specs=placed,
        out_specs=P("vec", ("parts", "leaf", "sub")),
        check_vma=False,
    )
```

```python
import functools

import jax
import jax.numpy as jnp
import numpy as np
from jax import lax
from jax.experimental import pallas as pl
from jax.experimental.pallas import tpu as pltpu
from jax.sharding import PartitionSpec as P

PTS = 256
RANK = 64
LEAVES = 32
NODES = 63
SLOTS = 8
REACH = 16
HALF = REACH * PTS
ROWS = 8
PAD = 16
GROUP = 4
WIDTH = 0.05
NEAR_WEIGHT = 0.0625
EMPTY = 3 * NODES
QUADS = 16
F32 = jnp.float32
BF16 = jnp.bfloat16
AXES = ("leaf", "sub")
NN = (((1,), (0,)), ((), ()))
NT = (((1,), (1,)), ((), ()))
TN = (((0,), (0,)), ((), ()))


def selections():
    source_part = (1, 1, 2, 2, 1, 3)
    target_part = (1, 2, 1, 2, 3, 1)
    source = np.zeros((64, 32), np.float32)
    target = np.zeros((32, 64), np.float32)
    for g in range(6):
        for c in range(3):
            source[(source_part[g] - 1) * 8 + c, 4 * g + c] = 1
            target[4 * g + c, (target_part[g] - 1) * 8 + c] = -2
        f = 4 * g + 3
        if g < 3:
            source[24 + 8 * g, f] = 1
            target[f, 48] = 1
        else:
            source[48, f] = 1
            target[f, 24 + 8 * (g - 3)] = 1
    source[48, 24] = 1
    target[24, 48] = 1
    return jnp.asarray(np.tile(source, (1, 4)), BF16), jnp.asarray(target, BF16)


def halves(x):
    high = x.astype(BF16)
    return high, (x - high.astype(F32)).astype(BF16)


def dot(a, b, dims=NN):
    return lax.dot_general(a, b, dims, preferred_element_type=F32)


def dot3(a, b, dims=NN):
    ah, al = halves(a)
    bh, bl = halves(b)
    rows = a.shape[0]
    both = dot(jnp.concatenate([ah, al], axis=0), bh, dims)
    return both[:rows] + both[rows:] + dot(ah, bl, dims)


def scaled(points):
    return (points - 0.5) * (1.0 / WIDTH)


def padded(points):
    return jnp.concatenate([points, jnp.zeros((5, points.shape[1]), F32)], axis=0)


def parts_of(c):
    n = c.shape[1]

    def rounded(x):
        return x.astype(BF16).astype(F32)

    p1 = rounded(c)
    rest = c - p1
    p2 = rounded(rest)
    p3 = rest - p2
    norm = jnp.broadcast_to(jnp.sum(c * c, axis=0, keepdims=True), (8, n))
    n1 = rounded(norm)
    rest = norm - n1
    n2 = rounded(rest)
    n3 = rest - n2
    rows = [p1, p2, p3, n1, n2, n3, jnp.ones((8, n), F32), jnp.zeros((8, n), F32)]
    return jnp.concatenate(rows, axis=0).astype(BF16)


def lower_lanes(rows):
    return lax.broadcasted_iota(jnp.int32, (rows, 128), 1) < RANK


def diagonal(x, vectors):
    return jnp.where(lower_lanes(vectors), x[:vectors], x[vectors:])


def spread_pair(pair):
    low = lower_lanes(pair.shape[0])
    zero = jnp.zeros_like(pair)
    return jnp.concatenate([jnp.where(low, pair, zero), jnp.where(low, zero, pair)], axis=0)


def pipelined(steps, first, second):
    for u in range(GROUP):
        first(u, u, 0)

    def body(i, carry):
        for h in range(2):
            base = (2 * i + h) * GROUP
            for u in range(GROUP):
                first(base + GROUP + u, u, 1 - h)
            for u in range(GROUP):
                second(base + u, u, h)
        return carry

    lax.fori_loop(0, (steps + 2 * GROUP - 1) // (2 * GROUP), body, 0)


class Copies:
    def __init__(self, sems):
        self.sems = sems
        self.count = 0

    def start(self, source, target):
        copy = pltpu.make_async_copy(source, target, self.sems.at[self.count])
        self.count += 1
        copy.start()
        return copy


def up_kernel(
    near_ref, far_ref, far_vec, charges_hbm, coords, basis_hbm, transfer_hbm,
    up_hbm, down_hbm, root_ref, local_ref, halo_ref, steps_ref, count_ref, entry_ref,
    charges, points, basis, transfer, coef, sems,
):
    vectors = charges.shape[0]
    start = Copies(sems).start
    quarter = LEAVES // 4
    in_charges, in_basis = [], []
    for i in range(4):
        lanes = slice(i * quarter * PTS, (i + 1) * quarter * PTS)
        leaves = slice(i * quarter, (i + 1) * quarter)
        in_charges.append(start(charges_hbm.at[:, lanes], charges.at[:, lanes]))
        in_basis.append(start(basis_hbm.at[leaves], basis.at[leaves]))
    in_transfer = start(transfer_hbm, transfer)
    device = lax.axis_index(AXES)
    first = device * LEAVES

    def scan_leaf(t, counts):
        here, there = counts
        for e in range(SLOTS):
            entry = near_ref[e, t]
            s = entry - first
            inside = jnp.logical_and(s >= 0, s < LEAVES)
            outside = jnp.logical_and(entry >= 0, jnp.logical_not(inside))
            local_ref[here] = t * 256 + s
            halo_ref[there] = t * 256 + jnp.where(s < 0, s + REACH, s - REACH)
            here = here + inside.astype(jnp.int32)
            there = there + outside.astype(jnp.int32)
        return here, there

    here, there = lax.fori_loop(0, LEAVES, scan_leaf, (jnp.int32(0), jnp.int32(0)))
    for u in range(PAD):
        local_ref[here + u] = LEAVES
        halo_ref[there + u] = LEAVES
    for q in range(QUADS):
        steps_ref[q] = q * 256 + 2 * q

    def scan_quad(q, count):
        top = far_ref[4, 4 * q]
        for e in range(4):
            for c in range(4):
                top = jnp.maximum(top, far_ref[4 + e, jnp.minimum(4 * q + c, NODES - 1)])
        steps_ref[count] = q * 256 + 2 * q + 1
        return count + (top >= 0).astype(jnp.int32)

    total = lax.fori_loop(0, QUADS, scan_quad, jnp.int32(QUADS))
    for u in range(PAD):
        steps_ref[total + u] = QUADS * 256
    count_ref[0] = here
    count_ref[1] = there
    count_ref[2] = total
    entry = far_vec[...]
    entry_ref[:, 0:NODES] = jnp.where(entry >= 0, entry - (device - 1) * NODES, EMPTY)
    entry_ref[:, NODES:64] = jnp.full((SLOTS, 1), EMPTY, jnp.int32)
    points[0:3] = coords[...]
    points[3:] = jnp.zeros((ROWS - 3, points.shape[1]), F32)

    out = [
        start(points.at[:, HALF:], up_hbm.at[2 * vectors :]),
        start(points.at[:, :HALF], down_hbm.at[2 * vectors :]),
    ]
    per = LEAVES // 8
    for p in range(LEAVES // 2):
        if p % per == 0:
            in_charges[p // per].wait()
            in_basis[p // per].wait()
            if p == per:
                out.append(start(charges.at[:, :HALF], down_hbm.at[0:vectors]))
            if p == 3 * per:
                out.append(start(charges.at[:, HALF:], up_hbm.at[0:vectors]))
        a, b = slice(2 * p * PTS, (2 * p + 1) * PTS), slice((2 * p + 1) * PTS, (2 * p + 2) * PTS)
        both = jnp.concatenate([charges[:, a], charges[:, b]], axis=0)
        value = diagonal(dot3(both, basis[2 * p : 2 * p + 2].reshape(2 * RANK, PTS), NT), vectors)
        coef[:, p * 128 : (p + 1) * 128] = value
    for hbm in (up_hbm, down_hbm):
        out.append(start(coef.at[:, :2048], hbm.at[vectors : 2 * vectors, :2048]))
    in_transfer.wait()
    for p in range(LEAVES // 2, LEAVES - 1):
        q = 2 * p - LEAVES
        both = jnp.concatenate(
            [coef[:, q * 128 : (q + 1) * 128], coef[:, (q + 1) * 128 : (q + 2) * 128]], axis=0
        )
        value = diagonal(dot3(both, transfer[q : q + 2].reshape(128, 128), NT), vectors)
        coef[:, p * 128 : (p + 1) * 128] = value
    root = dot3(coef[:, 30 * 128 : 31 * 128], transfer[30], NT)
    root = jnp.concatenate([root, jnp.zeros((vectors, RANK), F32)], axis=1)
    coef[:, 31 * 128 :] = root
    for hbm in (up_hbm, down_hbm):
        out.append(start(coef.at[:, 2048:], hbm.at[vectors : 2 * vectors, 2048:]))
    for g in range(root_ref.shape[0]):
        root_ref[g] = root
    for copy in out:
        copy.wait()


def source_tables(k, charges, points, select, sources, weights):
    parts = parts_of(points)
    sources[k] = dot(parts, select[:, 0:32], TN).astype(BF16)
    high, low = halves(charges)
    weights[k] = jnp.concatenate([high, low], axis=0)
    return parts


def near_steps(list_ref, sources, targets, weights, out_ref, tiles):
    vectors = out_ref.shape[0]
    highs = (tiles[:GROUP], tiles[GROUP : 2 * GROUP])
    lows = (tiles[2 * GROUP : 3 * GROUP], tiles[3 * GROUP :])

    def decode(j):
        code = list_ref[j]
        return lax.shift_right_logical(code, 8), jnp.bitwise_and(code, 255)

    def first(j, u, b):
        t, s = decode(j)
        high, low = halves(lax.rsqrt(dot(sources[s], targets[t])))
        highs[b][u][...] = high
        lows[b][u][...] = low

    def second(j, u, b):
        t, s = decode(j)
        q = weights[s]
        both = dot(q, highs[b][u][...])
        lanes = pl.ds(pl.multiple_of(t * PTS, PTS), PTS)
        out_ref[:, lanes] += both[:vectors] + both[vectors:] + dot(q[:vectors], lows[b][u][...])

    return first, second


def near_kernel(
    count_ref, list_ref, charges_hbm, coords, select, select_t,
    near_ref, targets_hbm,
    charges, targets, sources, weights, sems, *tiles,
):
    vectors = charges.shape[0]
    start = Copies(sems).start
    quarter = LEAVES // 4
    copies = []
    for i in range(4):
        lanes = slice(i * quarter * PTS, (i + 1) * quarter * PTS)
        copies.append(start(charges_hbm.at[:, lanes], charges.at[:, lanes]))
    near_ref[...] = jnp.zeros_like(near_ref)
    weights[LEAVES] = jnp.zeros((2 * vectors, PTS), BF16)
    for k in range(LEAVES):
        if k % quarter == 0:
            copies[k // quarter].wait()
        lanes = slice(k * PTS, (k + 1) * PTS)
        c = padded(scaled(coords[:, lanes]))
        parts = source_tables(k, charges[:, lanes], c, select, sources, weights)
        targets[k] = dot(select_t[...], parts).astype(BF16)
    sources[LEAVES] = sources[0]
    out = start(targets, targets_hbm)
    first, second = near_steps(list_ref, sources, targets, weights, near_ref, tiles)
    pipelined(count_ref[0], first, second)
    out.wait()


def down_kernel(
    groups, count_ref, list_ref, steps_ref, entry_ref,
    near_hbm, targets_hbm, lower_hbm, own_hbm, upper_hbm, basis_hbm, transfer_hbm,
    roots, skeleton, top_transfer, top_skeleton, select, select_t,
    out_hbm,
    near, targets, lower, own, upper, basis, transfer,
    sources, weights, nodes, pairs, feature, quads, coef_low, coef_high, local, top_coef,
    sems, *tiles,
):
    vectors = near.shape[0]
    device = lax.axis_index(AXES)
    low_mask = lower_lanes(vectors)
    coef_rows = slice(vectors, 2 * vectors)
    start = Copies(sems).start
    halo_in = []
    for hbm, vmem in ((lower_hbm, lower), (upper_hbm, upper)):
        halo_in.append(start(hbm.at[0:vectors], vmem.at[0:vectors]))
        halo_in.append(start(hbm.at[2 * vectors :], vmem.at[2 * vectors :]))
    near_in = [start(near_hbm, near), start(targets_hbm, targets)]
    coef_in = [
        start(hbm.at[coef_rows], vmem.at[coef_rows])
        for hbm, vmem in ((lower_hbm, lower), (own_hbm, own), (upper_hbm, upper))
    ]
    matrices_in = [start(transfer_hbm, transfer), start(basis_hbm, basis)]

    width = skeleton.shape[2]
    full = -(-width // 256) * 256
    raw = skeleton[...].reshape(3 * RANK, width)
    raw = jnp.concatenate([raw, jnp.zeros((3 * RANK, full - width), F32)], axis=1)
    shift = lax.rem(full - (device - 1) * NODES, full)
    window = pltpu.roll(raw, shift, 1)[:, :256]
    window = jnp.concatenate([scaled(window), jnp.zeros((RANK, 256), F32)], axis=0)
    window = window.T
    for i in range(2):
        nodes[i] = window[:, i * 128 : (i + 1) * 128]
    pairs[...] = jnp.zeros_like(pairs)
    for c in range(3):
        half = slice((c % 2) * RANK, (c % 2 + 1) * RANK)
        for base, first_node, count in ((0, 0, 96), (96, NODES, 32)):
            even = nodes[c // 2, pl.ds(first_node, count, stride=2), :][:, half]
            odd = nodes[c // 2, pl.ds(first_node + 1, count, stride=2), :][:, half]
            both = jnp.concatenate([even, odd], axis=1)
            pairs[pl.ds(base * 8 + c, count, stride=8), :] = both
    for g in range(24):
        c = jnp.concatenate([pairs[(4 * g + u) * 8 : (4 * g + u + 1) * 8] for u in range(4)], axis=1)
        value = dot(parts_of(c), select[...], TN).astype(BF16)
        feature[8 * g : 8 * g + 8] = value.reshape(8, RANK, 128)
    quad_lane = lax.broadcasted_iota(jnp.int32, (32, 256), 1) // RANK
    for q in range(QUADS):
        c = jnp.concatenate(
            [pairs[(96 + 2 * q + u) * 8 : (97 + 2 * q + u) * 8] for u in range(2)], axis=1
        )
        target = dot(select_t[...], parts_of(c))
        blocks = [jnp.where(quad_lane == i, target, 0.0) for i in range(4)]
        quads[q] = jnp.concatenate(blocks, axis=0).astype(BF16)

    for copy in halo_in:
        copy.wait()
    for k in range(LEAVES):
        buffer = lower if k < REACH else upper
        lanes = slice((k % REACH) * PTS, (k % REACH + 1) * PTS)
        c = padded(scaled(buffer[2 * vectors : 2 * vectors + 3, lanes]))
        source_tables(k, buffer[0:vectors, lanes], c, select, sources, weights)
    weights[LEAVES] = jnp.zeros((2 * vectors, PTS), BF16)
    sources[LEAVES] = sources[0]
    for copy in near_in:
        copy.wait()
    first, second = near_steps(list_ref, sources, targets, weights, near, tiles)
    pipelined(count_ref[1], first, second)

    for copy in coef_in:
        copy.wait()
    for b, buffer in enumerate((lower, own, upper)):
        for p in range(32):
            pair = buffer[coef_rows, p * 128 : (p + 1) * 128]
            swap = pltpu.roll(pair, RANK, 1)
            zero = jnp.zeros_like(pair)
            for n, (a, c) in enumerate(((pair, swap), (swap, pair))):
                if 2 * p + n == NODES:
                    continue
                for table, value in (
                    (coef_low, jnp.where(low_mask, a, zero)),
                    (coef_high, jnp.where(low_mask, zero, c)),
                ):
                    high, low = halves(value)
                    table[b * NODES + 2 * p + n] = jnp.concatenate([high, low], axis=0)
    coef_low[EMPTY] = jnp.zeros((2 * vectors, 128), BF16)
    coef_high[EMPTY] = jnp.zeros((2 * vectors, 128), BF16)
    local[...] = jnp.zeros_like(local)
    highs = (tiles[:GROUP], tiles[GROUP : 2 * GROUP])
    lows = (tiles[2 * GROUP : 3 * GROUP], tiles[3 * GROUP :])
    lane_group = lax.broadcasted_iota(jnp.int32, (RANK, 128), 1) // 32

    def entries(j):
        code = steps_ref[j]
        target = lax.shift_right_logical(code, 8)
        chunk = jnp.bitwise_and(code, 255)
        q = lax.shift_right_logical(chunk, 1)
        slot = 4 * jnp.bitwise_and(chunk, 1)
        return target, q, [[entry_ref[slot + e, 4 * q + i] for e in range(4)] for i in range(4)]

    def far_first(j, u, b):
        target, q, picks = entries(j)
        rows = []
        for e in range(4):
            value = feature[picks[3][e]]
            for i in range(3):
                value = jnp.where(lane_group == i, feature[picks[i][e]], value)
            rows.append(value)
        high, low = halves(lax.rsqrt(dot(jnp.concatenate(rows, axis=0), quads[q])))
        highs[b][u][...] = high
        lows[b][u][...] = low

    def far_second(j, u, b):
        target, q, picks = entries(j)
        sides = []
        for s in picks:
            left = coef_low[s[0]] + coef_high[s[1]]
            right = coef_low[s[2]] + coef_high[s[3]]
            sides.append(jnp.concatenate([left, right], axis=1))
        high = jnp.concatenate([side[:vectors] for side in sides], axis=0)
        low = jnp.concatenate([side[vectors:] for side in sides], axis=0)
        both = dot(jnp.concatenate([high, low], axis=0), highs[b][u][...])
        value = both[: 4 * vectors] + both[4 * vectors :] + dot(high, lows[b][u][...])
        local[2 * target] += diagonal(value[: 2 * vectors, :128], vectors)
        local[2 * target + 1] += diagonal(value[2 * vectors :, 128:], vectors)

    pipelined(count_ref[2], far_first, far_second)

    bits = groups.bit_length() - 1
    offsets = []
    offset = 0
    for h in range(bits):
        count = groups >> h
        offsets.append(offset)
        for i in range(count // 2):
            if h == 0:
                pair = roots[2 * i] + pltpu.roll(roots[2 * i + 1], RANK, 1)
            else:
                row = groups - (groups >> (h - 1)) + 2 * i
                below = offsets[h - 1] + 2 * i
                both = top_coef[below : below + 2].reshape(2 * vectors, 128)
                matrix = top_transfer[row : row + 2].reshape(128, 128)
                pair = diagonal(dot3(both, matrix, NT), vectors)
            top_coef[offset + i] = pair
        offset += count // 2
    upper_row = lax.broadcasted_iota(jnp.int32, (128, 128), 0) < RANK
    upper_lane = lax.broadcasted_iota(jnp.int32, (128, 128), 1) < RANK
    couple = []
    for h in range(bits):
        node = device // 2**h
        i = node // 2
        if h == 0:
            rows = [
                jnp.concatenate(
                    [nodes[c // 2, r : r + 1, c % 2 * RANK : (c % 2 + 1) * RANK] for c in range(3)],
                    axis=0,
                )
                for r in (NODES - 1, 2 * NODES - 1, 3 * NODES - 1)
            ]
            odd = node % 2 == 1
            left = jnp.where(odd, rows[0], rows[1])
            right = jnp.where(odd, rows[1], rows[2])
        else:
            row = groups - (groups >> (h - 1))
            left = scaled(top_skeleton[row + 2 * i])
            right = scaled(top_skeleton[row + 2 * i + 1])
        parts = parts_of(padded(jnp.concatenate([left, right], axis=1)))
        source = dot(parts, select[:, 0:32], TN).astype(BF16)
        target = dot(select_t[...], parts).astype(BF16)
        tile = jnp.where(upper_row != upper_lane, lax.rsqrt(dot(source, target)), 0.0)
        couple.append(dot3(top_coef[offsets[h] + i], tile))
    top = couple[bits - 1]
    for h in range(bits - 2, -1, -1):
        parent = device // 2 ** (h + 1)
        mine = jnp.where(low_mask == (parent % 2 == 0), top, 0.0)
        row = groups - (groups >> h) + 2 * (parent // 2)
        matrix = top_transfer[pl.ds(row, 2)].reshape(128, 128)
        top = couple[h] + dot3(mine, matrix)
    top = jnp.where(device % 2 == 1, pltpu.roll(top, RANK, 1), top)

    matrices_in[0].wait()
    local[30] += dot3(jnp.where(low_mask, local[31] + top, 0.0)[:, :RANK], transfer[30])
    for p in range(30, 15, -1):
        q = 2 * p - LEAVES
        both = dot3(spread_pair(local[p]), transfer[q : q + 2].reshape(128, 128))
        local[q] += both[:vectors]
        local[q + 1] += both[vectors:]
    matrices_in[1].wait()
    out = []
    for p in range(LEAVES // 2):
        both = dot3(spread_pair(local[p]), basis[2 * p : 2 * p + 2].reshape(128, PTS))
        for c in range(2):
            lanes = slice((2 * p + c) * PTS, (2 * p + c + 1) * PTS)
            near[:, lanes] = both[c * vectors : (c + 1) * vectors] + NEAR_WEIGHT * near[:, lanes]
        if p % 4 == 3:
            lanes = slice((p - 3) * 2 * PTS, (p + 1) * 2 * PTS)
            out.append(start(near.at[:, lanes], out_hbm.at[:, lanes]))
    for copy in out:
        copy.wait()


def whole(count, space=pltpu.VMEM):
    return [pl.BlockSpec(memory_space=space)] * count


def on_device(
    charges, coordinates, near_lists, far_lists, leaf_basis, local_transfer,
    skeleton, top_transfer, top_skeleton,
):
    vectors = charges.shape[0]
    groups = lax.axis_size(AXES)
    points = LEAVES * PTS
    height = 2 * vectors + ROWS
    shape = jax.ShapeDtypeStruct
    select, select_t = selections()
    params = pltpu.CompilerParams(vmem_limit_bytes=56 << 20)
    smem = pltpu.SMEM
    vmem = pltpu.VMEM
    matrices = [vmem((LEAVES, RANK, PTS), F32), vmem((LEAVES - 1, RANK, 128), F32)]
    up, down, root, local_list, halo_list, steps, counts, entries = pl.pallas_call(
        up_kernel,
        out_shape=[
            shape((height, HALF), F32),
            shape((height, HALF), F32),
            shape((groups, vectors, 128), F32),
            shape((LEAVES * SLOTS + PAD,), jnp.int32),
            shape((LEAVES * SLOTS + PAD,), jnp.int32),
            shape((2 * QUADS + PAD,), jnp.int32),
            shape((3,), jnp.int32),
            shape((SLOTS, 64), jnp.int32),
        ],
        in_specs=whole(2, smem) + whole(1) + whole(1, pl.ANY) + whole(1) + whole(2, pl.ANY),
        out_specs=whole(2, pl.ANY) + whole(1) + whole(4, smem) + whole(1),
        scratch_shapes=[vmem((vectors, points), F32), vmem((ROWS, points), F32)]
        + matrices
        + [vmem((vectors, 32 * 128), F32), pltpu.SemaphoreType.DMA((20,))],
        compiler_params=params,
    )(near_lists.T, far_lists.T, far_lists.T, charges, coordinates, leaf_basis, local_transfer)

    upward = [(i, i + 1) for i in range(groups - 1)]
    lower = lax.ppermute(up, AXES, upward)
    upper = lax.ppermute(down, AXES, [(j, i) for i, j in upward])
    roots = lax.all_to_all(root, AXES, 0, 0)

    tiles = [vmem((PTS, PTS), BF16)] * (4 * GROUP)
    tables = [vmem((LEAVES + 1, PTS, 32), BF16), vmem((LEAVES + 1, 2 * vectors, PTS), BF16)]
    near, targets = pl.pallas_call(
        near_kernel,
        out_shape=[shape((vectors, points), F32), shape((LEAVES, 32, PTS), BF16)],
        in_specs=whole(2, smem) + whole(1, pl.ANY) + whole(3),
        out_specs=whole(1) + whole(1, pl.ANY),
        scratch_shapes=[vmem((vectors, points), F32), vmem((LEAVES, 32, PTS), BF16)]
        + tables
        + [pltpu.SemaphoreType.DMA((5,))]
        + tiles,
        compiler_params=params,
        cost_estimate=pl.CostEstimate(
            flops=192 * 3 * 2 * PTS**3, transcendentals=192 * PTS**2, bytes_accessed=4 << 20
        ),
    )(counts, local_list, charges, coordinates, select, select_t)

    return pl.pallas_call(
        functools.partial(down_kernel, groups),
        out_shape=shape((vectors, points), F32),
        in_specs=whole(4, smem) + whole(7, pl.ANY) + whole(6),
        out_specs=pl.BlockSpec(memory_space=pl.ANY),
        scratch_shapes=[vmem((vectors, points), F32), vmem((LEAVES, 32, PTS), BF16)]
        + [vmem((height, HALF), F32)] * 3
        + matrices
        + tables
        + [
            vmem((2, 256, 128), F32),
            vmem((128 * 8, 128), F32),
            vmem((192, RANK, 128), BF16),
            vmem((QUADS, 128, 256), BF16),
            vmem((EMPTY + 1, 2 * vectors, 128), BF16),
            vmem((EMPTY + 1, 2 * vectors, 128), BF16),
            vmem((2 * QUADS + 2, vectors, 128), F32),
            vmem((groups, vectors, 128), F32),
            pltpu.SemaphoreType.DMA((16,)),
        ]
        + tiles,
        compiler_params=params,
    )(
        counts, halo_list, steps, entries, near, targets, lower, up, upper,
        leaf_basis, local_transfer, roots, skeleton.transpose(1, 2, 0),
        top_transfer, top_skeleton, select, select_t,
    )


def solution(mesh):
    placed = (
        P("vec", ("parts", "leaf", "sub")),
        P(None, ("parts", "leaf", "sub")),
        P(("parts", "leaf", "sub"), None),
        P(("parts", "leaf", "sub"), None),
        P(("parts", "leaf", "sub"), None, None),
        P(("parts", "leaf", "sub"), None, None),
        P("parts", None, None),
        P("parts", None, None),
        P("parts", None, None),
    )
    return jax.shard_map(
        on_device,
        mesh=mesh,
        in_specs=placed,
        out_specs=P("vec", ("parts", "leaf", "sub")),
        check_vma=False,
    )
```

```python
import functools

import jax
import jax.numpy as jnp
import numpy as np
from jax import lax
from jax.experimental import pallas as pl
from jax.experimental.pallas import tpu as pltpu
from jax.sharding import PartitionSpec as P

PTS = 256
RANK = 64
LEAVES = 32
NODES = 63
SLOTS = 8
REACH = 16
HALF = REACH * PTS
ROWS = 8
PAD = 16
HALO = LEAVES * SLOTS + PAD
STEPS = 2 * HALO
COUNTS = STEPS + 48
LISTS = COUNTS + 16
LOCAL_GROUP = 6
GROUP = 4
WIDTH = 0.05
NEAR_WEIGHT = 0.0625
EMPTY = 3 * NODES
QUADS = 16
F32 = jnp.float32
BF16 = jnp.bfloat16
AXES = ("leaf", "sub")
NN = (((1,), (0,)), ((), ()))
NT = (((1,), (1,)), ((), ()))
TN = (((0,), (0,)), ((), ()))


def selections():
    source_part = (1, 1, 2, 2, 1, 3)
    target_part = (1, 2, 1, 2, 3, 1)
    source = np.zeros((64, 32), np.float32)
    target = np.zeros((32, 64), np.float32)
    for g in range(6):
        for c in range(3):
            source[(source_part[g] - 1) * 8 + c, 4 * g + c] = 1
            target[4 * g + c, (target_part[g] - 1) * 8 + c] = -2
        f = 4 * g + 3
        if g < 3:
            source[24 + 8 * g, f] = 1
            target[f, 48] = 1
        else:
            source[48, f] = 1
            target[f, 24 + 8 * (g - 3)] = 1
    source[48, 24] = 1
    target[24, 48] = 1
    return jnp.asarray(np.tile(source, (1, 4)), BF16), jnp.asarray(target, BF16)


def halves(x):
    high = x.astype(BF16)
    return high, (x - high.astype(F32)).astype(BF16)


def dot(a, b, dims=NN):
    return lax.dot_general(a, b, dims, preferred_element_type=F32)


def dot3(a, b, dims=NN):
    ah, al = halves(a)
    bh, bl = halves(b)
    rows = a.shape[0]
    both = dot(jnp.concatenate([ah, al], axis=0), bh, dims)
    return both[:rows] + both[rows:] + dot(ah, bl, dims)


def scaled(points):
    return (points - 0.5) * (1.0 / WIDTH)


def padded(points):
    return jnp.concatenate([points, jnp.zeros((5, points.shape[1]), F32)], axis=0)


def parts_of(c):
    n = c.shape[1]

    def rounded(x):
        return x.astype(BF16).astype(F32)

    p1 = rounded(c)
    rest = c - p1
    p2 = rounded(rest)
    p3 = rest - p2
    norm = jnp.broadcast_to(jnp.sum(c * c, axis=0, keepdims=True), (8, n))
    n1 = rounded(norm)
    rest = norm - n1
    n2 = rounded(rest)
    n3 = rest - n2
    rows = [p1, p2, p3, n1, n2, n3, jnp.ones((8, n), F32), jnp.zeros((8, n), F32)]
    return jnp.concatenate(rows, axis=0).astype(BF16)


def lower_lanes(rows):
    return lax.broadcasted_iota(jnp.int32, (rows, 128), 1) < RANK


def diagonal(x, vectors):
    return jnp.where(lower_lanes(vectors), x[:vectors], x[vectors:])


def spread_pair(pair):
    low = lower_lanes(pair.shape[0])
    zero = jnp.zeros_like(pair)
    return jnp.concatenate([jnp.where(low, pair, zero), jnp.where(low, zero, pair)], axis=0)


def pipelined(steps, group, first, second):
    def both(base, h):
        for u in range(group):
            first(base + group + u, u, 1 - h)
        for u in range(group):
            second(base + u, u, h)

    def last(base, h):
        for u in range(group):
            second(base + u, u, h)

    for u in range(group):
        first(u, u, 0)
    more = jnp.maximum((steps + group - 1) // group, 1) - 1

    def body(i, carry):
        both(2 * i * group, 0)
        both((2 * i + 1) * group, 1)
        return carry

    lax.fori_loop(0, more // 2, body, 0)
    base = more // 2 * 2 * group

    @pl.when(more % 2 == 1)
    def _():
        both(base, 0)
        last(base + group, 1)

    @pl.when(more % 2 == 0)
    def _():
        last(base, 0)


class Copies:
    def __init__(self, sems):
        self.sems = sems
        self.count = 0

    def start(self, source, target):
        copy = pltpu.make_async_copy(source, target, self.sems.at[self.count])
        self.count += 1
        copy.start()
        return copy


def up_kernel(
    near_hbm, far_hbm, charges_hbm, coords_hbm, basis_hbm, transfer_hbm,
    up_hbm, down_hbm, root_hbm, list_hbm, entry_hbm,
    near_ref, far_ref, far_vec, coords, root_ref, list_ref, entry_ref,
    charges, points, basis, transfer, coef, sems,
):
    vectors = charges.shape[0]
    start = Copies(sems).start
    quarter = LEAVES // 4
    in_lists = [start(near_hbm, near_ref), start(far_hbm, far_ref)]
    in_vectors = [start(far_hbm, far_vec), start(coords_hbm, coords)]
    incoming = []

    def fetch(i):
        lanes = slice(i * quarter * PTS, (i + 1) * quarter * PTS)
        leaves = slice(i * quarter, (i + 1) * quarter)
        incoming.append(start(charges_hbm.at[:, lanes], charges.at[:, lanes]))
        incoming.append(start(basis_hbm.at[leaves], basis.at[leaves]))

    for i in range(4):
        fetch(i)
    in_transfer = start(transfer_hbm, transfer)
    device = lax.axis_index(AXES)
    first = device * LEAVES
    for copy in in_lists:
        copy.wait()

    def scan_leaf(t, counts):
        here, there = counts
        for e in range(SLOTS):
            entry = near_ref[e, t]
            s = entry - first
            inside = jnp.logical_and(s >= 0, s < LEAVES)
            outside = jnp.logical_and(entry >= 0, jnp.logical_not(inside))
            list_ref[here] = t * 256 + s
            list_ref[there] = t * 256 + jnp.where(s < 0, s + REACH, s - REACH)
            here = here + inside.astype(jnp.int32)
            there = there + outside.astype(jnp.int32)
        return here, there

    here, there = lax.fori_loop(0, LEAVES, scan_leaf, (jnp.int32(0), jnp.int32(HALO)))
    for u in range(PAD):
        list_ref[here + u] = LEAVES
        list_ref[there + u] = LEAVES
    for q in range(QUADS):
        list_ref[STEPS + q] = q * 256 + 2 * q

    def scan_quad(q, count):
        top = far_ref[4, 4 * q]
        for e in range(4):
            for c in range(4):
                top = jnp.maximum(top, far_ref[4 + e, jnp.minimum(4 * q + c, NODES - 1)])
        list_ref[count] = q * 256 + 2 * q + 1
        return count + (top >= 0).astype(jnp.int32)

    total = lax.fori_loop(0, QUADS, scan_quad, jnp.int32(STEPS + QUADS))
    for u in range(PAD):
        list_ref[total + u] = QUADS * 256
    list_ref[COUNTS] = here
    list_ref[COUNTS + 1] = there - HALO
    list_ref[COUNTS + 2] = total - STEPS
    for copy in in_vectors:
        copy.wait()
    entry = far_vec[...]
    entry_ref[:, 0:NODES] = jnp.where(entry >= 0, entry - (device - 1) * NODES, EMPTY)
    entry_ref[:, NODES:64] = jnp.full((SLOTS, 1), EMPTY, jnp.int32)
    points[0:3] = coords[...]
    points[3:] = jnp.zeros((ROWS - 3, points.shape[1]), F32)

    out = [
        start(list_ref, list_hbm),
        start(entry_ref, entry_hbm),
        start(points.at[:, HALF:], up_hbm.at[2 * vectors :]),
        start(points.at[:, :HALF], down_hbm.at[2 * vectors :]),
    ]
    per = LEAVES // 8
    for p in range(LEAVES // 2):
        if p % per == 0:
            i = p // per
            incoming[2 * i].wait()
            incoming[2 * i + 1].wait()
            if p == per:
                out.append(start(charges.at[:, :HALF], down_hbm.at[0:vectors]))
            if p == 3 * per:
                out.append(start(charges.at[:, HALF:], up_hbm.at[0:vectors]))
        a, b = slice(2 * p * PTS, (2 * p + 1) * PTS), slice((2 * p + 1) * PTS, (2 * p + 2) * PTS)
        both = jnp.concatenate([charges[:, a], charges[:, b]], axis=0)
        value = diagonal(dot3(both, basis[2 * p : 2 * p + 2].reshape(2 * RANK, PTS), NT), vectors)
        coef[:, p * 128 : (p + 1) * 128] = value
    for hbm in (up_hbm, down_hbm):
        out.append(start(coef.at[:, :2048], hbm.at[vectors : 2 * vectors, :2048]))
    in_transfer.wait()
    for p in range(LEAVES // 2, LEAVES - 1):
        q = 2 * p - LEAVES
        both = jnp.concatenate(
            [coef[:, q * 128 : (q + 1) * 128], coef[:, (q + 1) * 128 : (q + 2) * 128]], axis=0
        )
        value = diagonal(dot3(both, transfer[q : q + 2].reshape(128, 128), NT), vectors)
        coef[:, p * 128 : (p + 1) * 128] = value
    root = dot3(coef[:, 30 * 128 : 31 * 128], transfer[30], NT)
    root = jnp.concatenate([root, jnp.zeros((vectors, RANK), F32)], axis=1)
    coef[:, 31 * 128 :] = root
    for hbm in (up_hbm, down_hbm):
        out.append(start(coef.at[:, 2048:], hbm.at[vectors : 2 * vectors, 2048:]))
    for g in range(root_ref.shape[0]):
        root_ref[g] = root
    out.append(start(root_ref, root_hbm))
    for copy in out:
        copy.wait()


def source_tables(k, charges, points, select, sources, weights):
    parts = parts_of(points)
    sources[k] = dot(parts, select[:, 0:32], TN).astype(BF16)
    high, low = halves(charges)
    weights[k] = jnp.concatenate([high, low], axis=0)
    return parts


def empty_source(sources, weights):
    weights[LEAVES] = jnp.zeros(weights.shape[1:], BF16)
    sources[LEAVES] = sources[0]


def near_steps(list_ref, base, targets, tables, out_ref, highs, lows):
    sources, weights = tables
    vectors = out_ref.shape[0]

    def decode(j):
        code = list_ref[base + j]
        return lax.shift_right_logical(code, 8), jnp.bitwise_and(code, 255)

    def first(j, u, b):
        t, s = decode(j)
        high, low = halves(lax.rsqrt(dot(sources[s], targets[t])))
        highs[b][u][...] = high
        lows[b][u][...] = low

    def second(j, u, b):
        t, s = decode(j)
        q = weights[s]
        both = dot(q, highs[b][u][...])
        lanes = pl.ds(pl.multiple_of(t * PTS, PTS), PTS)
        out_ref[:, lanes] += both[:vectors] + both[vectors:] + dot(q[:vectors], lows[b][u][...])

    return first, second


def near_kernel(
    list_hbm, charges_hbm, coords_hbm, select_hbm, select_t_hbm,
    near_hbm, targets_hbm,
    list_ref, coords, select, select_t, near_ref,
    charges, targets, *rest,
):
    tables, sems, tiles = rest[:2], rest[2], rest[3:]
    highs = (tiles[:LOCAL_GROUP], tiles[LOCAL_GROUP : 2 * LOCAL_GROUP])
    lows = (tiles[2 * LOCAL_GROUP : 3 * LOCAL_GROUP], tiles[3 * LOCAL_GROUP :])
    start = Copies(sems).start
    quarter = LEAVES // 4
    small = [start(coords_hbm, coords), start(select_hbm, select), start(select_t_hbm, select_t)]
    copies = []
    for i in range(4):
        lanes = slice(i * quarter * PTS, (i + 1) * quarter * PTS)
        copies.append(start(charges_hbm.at[:, lanes], charges.at[:, lanes]))
    in_list = start(list_hbm, list_ref)
    near_ref[...] = jnp.zeros_like(near_ref)
    for copy in small:
        copy.wait()
    for k in range(LEAVES):
        if k % quarter == 0:
            copies[k // quarter].wait()
        lanes = slice(k * PTS, (k + 1) * PTS)
        c = padded(scaled(coords[:, lanes]))
        parts = source_tables(k, charges[:, lanes], c, select, *tables)
        targets[k] = dot(select_t[...], parts).astype(BF16)
    empty_source(*tables)
    out = start(targets, targets_hbm)
    in_list.wait()
    first, second = near_steps(list_ref, 0, targets, tables, near_ref, highs, lows)
    pipelined(list_ref[COUNTS], LOCAL_GROUP, first, second)
    out_near = start(near_ref, near_hbm)
    out.wait()
    out_near.wait()


def down_kernel(
    groups, list_hbm, entry_hbm,
    near_hbm, targets_hbm, lower_hbm, own_hbm, upper_hbm, basis_hbm, transfer_hbm,
    roots_hbm, skeleton_hbm, top_transfer_hbm, top_skeleton_hbm, select_hbm, select_t_hbm,
    out_hbm,
    list_ref, entry_ref, roots, skeleton, top_transfer, top_skeleton, select, select_t,
    near, near_local, targets, lower, own, upper, basis, transfer,
    sources, weights,
    nodes, pairs, feature, quads, coef_low, coef_high, local, top_coef,
    sems, *tiles,
):
    tables = (sources, weights)
    highs = (tiles[:GROUP], tiles[GROUP : 2 * GROUP])
    lows = (tiles[2 * GROUP : 3 * GROUP], tiles[3 * GROUP :])
    vectors = near.shape[0]
    device = lax.axis_index(AXES)
    low_mask = lower_lanes(vectors)
    coef_rows = slice(vectors, 2 * vectors)
    start = Copies(sems).start
    skeleton_in = [
        start(skeleton_hbm, skeleton),
        start(select_hbm, select),
        start(select_t_hbm, select_t),
    ]
    for copy in skeleton_in:
        copy.wait()
    halo_in = [
        start(roots_hbm, roots),
        start(top_transfer_hbm, top_transfer),
        start(top_skeleton_hbm, top_skeleton),
        start(list_hbm, list_ref),
        start(entry_hbm, entry_ref),
    ]
    for hbm, vmem in ((lower_hbm, lower), (upper_hbm, upper)):
        halo_in.append(start(hbm.at[0:vectors], vmem.at[0:vectors]))
        halo_in.append(start(hbm.at[2 * vectors :], vmem.at[2 * vectors :]))

    width = skeleton.shape[2]
    full = -(-width // 256) * 256
    raw = skeleton[...].reshape(3 * RANK, width)
    raw = jnp.concatenate([raw, jnp.zeros((3 * RANK, full - width), F32)], axis=1)
    shift = lax.rem(full - (device - 1) * NODES, full)
    window = pltpu.roll(raw, shift, 1)[:, :256]
    window = jnp.concatenate([scaled(window), jnp.zeros((RANK, 256), F32)], axis=0)
    window = window.T
    for i in range(2):
        nodes[i] = window[:, i * 128 : (i + 1) * 128]
    pairs[...] = jnp.zeros_like(pairs)
    for c in range(3):
        half = slice((c % 2) * RANK, (c % 2 + 1) * RANK)
        for base, first_node, count in ((0, 0, 96), (96, NODES, 32)):
            even = nodes[c // 2, pl.ds(first_node, count, stride=2), :][:, half]
            odd = nodes[c // 2, pl.ds(first_node + 1, count, stride=2), :][:, half]
            both = jnp.concatenate([even, odd], axis=1)
            pairs[pl.ds(base * 8 + c, count, stride=8), :] = both
    for g in range(24):
        c = jnp.concatenate([pairs[(4 * g + u) * 8 : (4 * g + u + 1) * 8] for u in range(4)], axis=1)
        value = dot(parts_of(c), select[...], TN).astype(BF16)
        feature[8 * g : 8 * g + 8] = value.reshape(8, RANK, 128)
    quad_lane = lax.broadcasted_iota(jnp.int32, (32, 256), 1) // RANK
    for q in range(QUADS):
        c = jnp.concatenate(
            [pairs[(96 + 2 * q + u) * 8 : (97 + 2 * q + u) * 8] for u in range(2)], axis=1
        )
        target = dot(select_t[...], parts_of(c))
        blocks = [jnp.where(quad_lane == i, target, 0.0) for i in range(4)]
        quads[q] = jnp.concatenate(blocks, axis=0).astype(BF16)

    for copy in halo_in:
        copy.wait()
    coef_in = [start(targets_hbm, targets)]
    for hbm, vmem in ((lower_hbm, lower), (own_hbm, own), (upper_hbm, upper)):
        coef_in.append(start(hbm.at[coef_rows], vmem.at[coef_rows]))
    bits = groups.bit_length() - 1
    offsets = []
    offset = 0
    for h in range(bits):
        count = groups >> h
        offsets.append(offset)
        for i in range(count // 2):
            if h == 0:
                pair = roots[2 * i] + pltpu.roll(roots[2 * i + 1], RANK, 1)
            else:
                row = groups - (groups >> (h - 1)) + 2 * i
                below = offsets[h - 1] + 2 * i
                both = top_coef[below : below + 2].reshape(2 * vectors, 128)
                matrix = top_transfer[row : row + 2].reshape(128, 128)
                pair = diagonal(dot3(both, matrix, NT), vectors)
            top_coef[offset + i] = pair
        offset += count // 2
    upper_row = lax.broadcasted_iota(jnp.int32, (128, 128), 0) < RANK
    upper_lane = lax.broadcasted_iota(jnp.int32, (128, 128), 1) < RANK
    couple = []
    for h in range(bits):
        node = device // 2**h
        i = node // 2
        if h == 0:
            rows = [
                jnp.concatenate(
                    [nodes[c // 2, r : r + 1, c % 2 * RANK : (c % 2 + 1) * RANK] for c in range(3)],
                    axis=0,
                )
                for r in (NODES - 1, 2 * NODES - 1, 3 * NODES - 1)
            ]
            odd = node % 2 == 1
            left = jnp.where(odd, rows[0], rows[1])
            right = jnp.where(odd, rows[1], rows[2])
        else:
            row = groups - (groups >> (h - 1))
            left = scaled(top_skeleton[row + 2 * i])
            right = scaled(top_skeleton[row + 2 * i + 1])
        parts = parts_of(padded(jnp.concatenate([left, right], axis=1)))
        source = dot(parts, select[:, 0:32], TN).astype(BF16)
        target = dot(select_t[...], parts).astype(BF16)
        tile = jnp.where(upper_row != upper_lane, lax.rsqrt(dot(source, target)), 0.0)
        couple.append(dot3(top_coef[offsets[h] + i], tile))
    top = couple[bits - 1]
    for h in range(bits - 2, -1, -1):
        parent = device // 2 ** (h + 1)
        mine = jnp.where(low_mask == (parent % 2 == 0), top, 0.0)
        row = groups - (groups >> h) + 2 * (parent // 2)
        matrix = top_transfer[pl.ds(row, 2)].reshape(128, 128)
        top = couple[h] + dot3(mine, matrix)
    top = jnp.where(device % 2 == 1, pltpu.roll(top, RANK, 1), top)

    for k in range(LEAVES):
        buffer = lower if k < REACH else upper
        lanes = slice((k % REACH) * PTS, (k % REACH + 1) * PTS)
        c = padded(scaled(buffer[2 * vectors : 2 * vectors + 3, lanes]))
        source_tables(k, buffer[0:vectors, lanes], c, select, *tables)
    empty_source(*tables)
    for copy in coef_in:
        copy.wait()
    late_in = [start(transfer_hbm, transfer), start(basis_hbm, basis), start(near_hbm, near_local)]
    near[...] = jnp.zeros_like(near)
    for b, buffer in enumerate((lower, own, upper)):
        for p in range(32):
            pair = buffer[coef_rows, p * 128 : (p + 1) * 128]
            swap = pltpu.roll(pair, RANK, 1)
            zero = jnp.zeros_like(pair)
            for n, (a, c) in enumerate(((pair, swap), (swap, pair))):
                if 2 * p + n == NODES:
                    continue
                for table, value in (
                    (coef_low, jnp.where(low_mask, a, zero)),
                    (coef_high, jnp.where(low_mask, zero, c)),
                ):
                    high, low = halves(value)
                    table[b * NODES + 2 * p + n] = jnp.concatenate([high, low], axis=0)
    coef_low[EMPTY] = jnp.zeros((2 * vectors, 128), BF16)
    coef_high[EMPTY] = jnp.zeros((2 * vectors, 128), BF16)
    local[...] = jnp.zeros_like(local)
    lane_group = lax.broadcasted_iota(jnp.int32, (RANK, 128), 1) // 32

    def entries(j):
        code = list_ref[STEPS + j]
        target = lax.shift_right_logical(code, 8)
        chunk = jnp.bitwise_and(code, 255)
        q = lax.shift_right_logical(chunk, 1)
        slot = 4 * jnp.bitwise_and(chunk, 1)
        return target, q, [[entry_ref[slot + e, 4 * q + i] for e in range(4)] for i in range(4)]

    def far_first(j, u, b):
        target, q, picks = entries(j)
        rows = []
        for e in range(4):
            value = feature[picks[3][e]]
            for i in range(3):
                value = jnp.where(lane_group == i, feature[picks[i][e]], value)
            rows.append(value)
        high, low = halves(lax.rsqrt(dot(jnp.concatenate(rows, axis=0), quads[q])))
        highs[b][u][...] = high
        lows[b][u][...] = low

    def far_second(j, u, b):
        target, q, picks = entries(j)
        sides = []
        for s in picks:
            left = coef_low[s[0]] + coef_high[s[1]]
            right = coef_low[s[2]] + coef_high[s[3]]
            sides.append(jnp.concatenate([left, right], axis=1))
        high = jnp.concatenate([side[:vectors] for side in sides], axis=0)
        low = jnp.concatenate([side[vectors:] for side in sides], axis=0)
        both = dot(jnp.concatenate([high, low], axis=0), highs[b][u][...])
        value = both[: 4 * vectors] + both[4 * vectors :] + dot(high, lows[b][u][...])
        local[2 * target] += diagonal(value[: 2 * vectors, :128], vectors)
        local[2 * target + 1] += diagonal(value[2 * vectors :, 128:], vectors)

    first, second = near_steps(list_ref, HALO, targets, tables, near, highs, lows)
    pipelined(list_ref[COUNTS + 1], GROUP, first, second)
    pipelined(list_ref[COUNTS + 2], GROUP, far_first, far_second)

    for copy in late_in:
        copy.wait()
    local[30] += dot3(jnp.where(low_mask, local[31] + top, 0.0)[:, :RANK], transfer[30])
    for p in range(30, 15, -1):
        q = 2 * p - LEAVES
        both = dot3(spread_pair(local[p]), transfer[q : q + 2].reshape(128, 128))
        local[q] += both[:vectors]
        local[q + 1] += both[vectors:]
    out = []
    for p in range(LEAVES // 2):
        both = dot3(spread_pair(local[p]), basis[2 * p : 2 * p + 2].reshape(128, PTS))
        for c in range(2):
            lanes = slice((2 * p + c) * PTS, (2 * p + c + 1) * PTS)
            close = near[:, lanes] + near_local[:, lanes]
            near[:, lanes] = both[c * vectors : (c + 1) * vectors] + NEAR_WEIGHT * close
        if p % 4 == 3:
            lanes = slice((p - 3) * 2 * PTS, (p + 1) * 2 * PTS)
            out.append(start(near.at[:, lanes], out_hbm.at[:, lanes]))
    for copy in out:
        copy.wait()


def whole(count, space=pltpu.VMEM):
    return [pl.BlockSpec(memory_space=space)] * count


def on_device(
    charges, coordinates, near_lists, far_lists, leaf_basis, local_transfer,
    skeleton, top_transfer, top_skeleton,
):
    vectors = charges.shape[0]
    groups = lax.axis_size(AXES)
    points = LEAVES * PTS
    height = 2 * vectors + ROWS
    shape = jax.ShapeDtypeStruct
    select, select_t = selections()
    params = pltpu.CompilerParams(vmem_limit_bytes=(64 << 20) - (64 << 10))
    smem = pltpu.SMEM
    vmem = pltpu.VMEM
    matrices = [vmem((LEAVES, RANK, PTS), F32), vmem((LEAVES - 1, RANK, 128), F32)]
    list_shape = (LISTS,)
    up, down, root, lists, entries = pl.pallas_call(
        up_kernel,
        out_shape=[
            shape((height, HALF), F32),
            shape((height, HALF), F32),
            shape((groups, vectors, 128), F32),
            shape(list_shape, jnp.int32),
            shape((SLOTS, 64), jnp.int32),
        ],
        in_specs=whole(6, pl.ANY),
        out_specs=whole(5, pl.ANY),
        scratch_shapes=[
            smem((SLOTS, LEAVES), jnp.int32),
            smem((SLOTS, NODES), jnp.int32),
            vmem((SLOTS, NODES), jnp.int32),
            vmem((3, points), F32),
            vmem((groups, vectors, 128), F32),
            smem(list_shape, jnp.int32),
            vmem((SLOTS, 64), jnp.int32),
            vmem((vectors, points), F32),
            vmem((ROWS, points), F32),
        ]
        + matrices
        + [vmem((vectors, 32 * 128), F32), pltpu.SemaphoreType.DMA((24,))],
        compiler_params=params,
    )(near_lists.T, far_lists.T, charges, coordinates, leaf_basis, local_transfer)

    upward = [(i, i + 1) for i in range(groups - 1)]
    lower = lax.ppermute(up, AXES, upward)
    upper = lax.ppermute(down, AXES, [(j, i) for i, j in upward])
    roots = lax.all_to_all(root, AXES, 0, 0)

    tile = vmem((PTS, PTS), BF16)
    tables = [
        vmem((LEAVES + 1, PTS, 32), BF16),
        vmem((LEAVES + 1, 2 * vectors, PTS), BF16),
    ]
    selects = [vmem(select.shape, BF16), vmem(select_t.shape, BF16)]
    near, targets = pl.pallas_call(
        near_kernel,
        out_shape=[shape((vectors, points), F32), shape((LEAVES, 32, PTS), BF16)],
        in_specs=whole(5, pl.ANY),
        out_specs=whole(2, pl.ANY),
        scratch_shapes=[smem(list_shape, jnp.int32), vmem((3, points), F32)]
        + selects
        + [vmem((vectors, points), F32)] * 2
        + [vmem((LEAVES, 32, PTS), BF16)]
        + tables
        + [pltpu.SemaphoreType.DMA((10,))]
        + [tile] * (4 * LOCAL_GROUP),
        compiler_params=params,
        cost_estimate=pl.CostEstimate(
            flops=192 * 3 * 2 * PTS**3, transcendentals=192 * PTS**2, bytes_accessed=4 << 20
        ),
    )(lists, charges, coordinates, select, select_t)

    skeletons = skeleton.transpose(1, 2, 0)
    return pl.pallas_call(
        functools.partial(down_kernel, groups),
        out_shape=shape((vectors, points), F32),
        in_specs=whole(15, pl.ANY),
        out_specs=pl.BlockSpec(memory_space=pl.ANY),
        scratch_shapes=[
            smem(list_shape, jnp.int32),
            smem((SLOTS, 64), jnp.int32),
            vmem((groups, vectors, 128), F32),
            vmem(skeletons.shape, F32),
            vmem(top_transfer.shape, F32),
            vmem(top_skeleton.shape, F32),
        ]
        + selects
        + [vmem((vectors, points), F32)] * 2
        + [vmem((LEAVES, 32, PTS), BF16)]
        + [vmem((height, HALF), F32)] * 3
        + matrices
        + tables
        + [
            vmem((2, 256, 128), F32),
            vmem((128 * 8, 128), F32),
            vmem((192, RANK, 128), BF16),
            vmem((QUADS, 128, 256), BF16),
            vmem((EMPTY + 1, 2 * vectors, 128), BF16),
            vmem((EMPTY + 1, 2 * vectors, 128), BF16),
            vmem((2 * QUADS + 2, vectors, 128), F32),
            vmem((groups, vectors, 128), F32),
            pltpu.SemaphoreType.DMA((24,)),
        ]
        + [tile] * (4 * GROUP),
        compiler_params=params,
    )(
        lists, entries, near, targets, lower, up, upper, leaf_basis, local_transfer,
        roots, skeletons, top_transfer, top_skeleton, select, select_t,
    )


def solution(mesh):
    placed = (
        P("vec", ("parts", "leaf", "sub")),
        P(None, ("parts", "leaf", "sub")),
        P(("parts", "leaf", "sub"), None),
        P(("parts", "leaf", "sub"), None),
        P(("parts", "leaf", "sub"), None, None),
        P(("parts", "leaf", "sub"), None, None),
        P("parts", None, None),
        P("parts", None, None),
        P("parts", None, None),
    )
    return jax.shard_map(
        on_device,
        mesh=mesh,
        in_specs=placed,
        out_specs=P("vec", ("parts", "leaf", "sub")),
        check_vma=False,
    )
```

```python
import functools

import jax
import jax.numpy as jnp
import numpy as np
from jax import lax
from jax.experimental import pallas as pl
from jax.experimental.pallas import tpu as pltpu
from jax.sharding import PartitionSpec as P

PTS = 256
RANK = 64
LEAVES = 32
NODES = 63
SLOTS = 8
REACH = 16
HALF = REACH * PTS
ROWS = 8
PAD = 16
HALO = LEAVES * SLOTS + PAD
STEPS = 2 * HALO
COUNTS = STEPS + 48
LISTS = COUNTS + 16
LOCAL_GROUP = 6
GROUP = 4
WIDTH = 0.05
NEAR_WEIGHT = 0.0625
EMPTY = 3 * NODES
QUADS = 16
F32 = jnp.float32
BF16 = jnp.bfloat16
AXES = ("leaf", "sub")
NN = (((1,), (0,)), ((), ()))
NT = (((1,), (1,)), ((), ()))
TN = (((0,), (0,)), ((), ()))


def selections():
    source_part = (1, 1, 2, 2, 1, 3)
    target_part = (1, 2, 1, 2, 3, 1)
    source = np.zeros((64, 32), np.float32)
    target = np.zeros((32, 64), np.float32)
    for g in range(6):
        for c in range(3):
            source[(source_part[g] - 1) * 8 + c, 4 * g + c] = 1
            target[4 * g + c, (target_part[g] - 1) * 8 + c] = -2
        f = 4 * g + 3
        if g < 3:
            source[24 + 8 * g, f] = 1
            target[f, 48] = 1
        else:
            source[48, f] = 1
            target[f, 24 + 8 * (g - 3)] = 1
    source[48, 24] = 1
    target[24, 48] = 1
    return jnp.asarray(np.tile(source, (1, 4)), BF16), jnp.asarray(target, BF16)


def halves(x):
    high = x.astype(BF16)
    return high, (x - high.astype(F32)).astype(BF16)


def dot(a, b, dims=NN):
    return lax.dot_general(a, b, dims, preferred_element_type=F32)


def dot3(a, b, dims=NN):
    ah, al = halves(a)
    bh, bl = halves(b)
    rows = a.shape[0]
    both = dot(jnp.concatenate([ah, al], axis=0), bh, dims)
    return both[:rows] + both[rows:] + dot(ah, bl, dims)


def scaled(points):
    return (points - 0.5) * (1.0 / WIDTH)


def padded(points):
    return jnp.concatenate([points, jnp.zeros((5, points.shape[1]), F32)], axis=0)


def parts_of(c):
    n = c.shape[1]

    def rounded(x):
        return x.astype(BF16).astype(F32)

    p1 = rounded(c)
    rest = c - p1
    p2 = rounded(rest)
    p3 = rest - p2
    norm = jnp.broadcast_to(jnp.sum(c * c, axis=0, keepdims=True), (8, n))
    n1 = rounded(norm)
    rest = norm - n1
    n2 = rounded(rest)
    n3 = rest - n2
    rows = [p1, p2, p3, n1, n2, n3, jnp.ones((8, n), F32), jnp.zeros((8, n), F32)]
    return jnp.concatenate(rows, axis=0).astype(BF16)


def lower_lanes(rows):
    return lax.broadcasted_iota(jnp.int32, (rows, 128), 1) < RANK


def diagonal(x, vectors):
    return jnp.where(lower_lanes(vectors), x[:vectors], x[vectors:])


def spread_pair(pair):
    low = lower_lanes(pair.shape[0])
    zero = jnp.zeros_like(pair)
    return jnp.concatenate([jnp.where(low, pair, zero), jnp.where(low, zero, pair)], axis=0)


def pipelined(begin, end, group, stages):
    def first(base, h):
        for u in range(group):
            for stage in stages:
                stage[0](base + u, u, h)

    def second(base, h):
        for u in range(group):
            for stage in stages:
                stage[1](base + u, u, h)

    def both(base, h):
        first(base + group, 1 - h)
        second(base, h)

    first(begin, 0)
    more = (end - begin) // group - 1

    def body(i, carry):
        base = begin + 2 * i * group
        both(base, 0)
        both(base + group, 1)
        return carry

    lax.fori_loop(0, more // 2, body, 0)
    base = begin + more // 2 * 2 * group

    @pl.when(more % 2 == 1)
    def _():
        both(base, 0)
        second(base + group, 1)

    @pl.when(more % 2 == 0)
    def _():
        second(base, 0)


class Copies:
    def __init__(self, sems):
        self.sems = sems
        self.count = 0

    def start(self, source, target):
        copy = pltpu.make_async_copy(source, target, self.sems.at[self.count])
        self.count += 1
        copy.start()
        return copy


def up_kernel(
    charges_hbm, coords_hbm, basis_hbm, transfer_hbm,
    up_hbm, down_hbm, root_hbm,
    coords, root_ref,
    charges, points, basis, transfer, coef, sems,
):
    vectors = charges.shape[0]
    start = Copies(sems).start
    quarter = LEAVES // 4
    in_coords = start(coords_hbm, coords)
    incoming = []

    def fetch(i):
        lanes = slice(i * quarter * PTS, (i + 1) * quarter * PTS)
        leaves = slice(i * quarter, (i + 1) * quarter)
        incoming.append(start(charges_hbm.at[:, lanes], charges.at[:, lanes]))
        incoming.append(start(basis_hbm.at[leaves], basis.at[leaves]))

    for i in range(4):
        fetch(i)
    in_transfer = start(transfer_hbm, transfer)
    in_coords.wait()
    points[0:3] = coords[...]
    points[3:] = jnp.zeros((ROWS - 3, points.shape[1]), F32)

    out = [
        start(points.at[:, HALF:], up_hbm.at[2 * vectors :]),
        start(points.at[:, :HALF], down_hbm.at[2 * vectors :]),
    ]
    per = LEAVES // 8
    for p in range(LEAVES // 2):
        if p % per == 0:
            i = p // per
            incoming[2 * i].wait()
            incoming[2 * i + 1].wait()
            if p == per:
                out.append(start(charges.at[:, :HALF], down_hbm.at[0:vectors]))
            if p == 3 * per:
                out.append(start(charges.at[:, HALF:], up_hbm.at[0:vectors]))
        a, b = slice(2 * p * PTS, (2 * p + 1) * PTS), slice((2 * p + 1) * PTS, (2 * p + 2) * PTS)
        both = jnp.concatenate([charges[:, a], charges[:, b]], axis=0)
        value = diagonal(dot3(both, basis[2 * p : 2 * p + 2].reshape(2 * RANK, PTS), NT), vectors)
        coef[:, p * 128 : (p + 1) * 128] = value
    for hbm in (up_hbm, down_hbm):
        out.append(start(coef.at[:, :2048], hbm.at[vectors : 2 * vectors, :2048]))
    in_transfer.wait()
    for p in range(LEAVES // 2, LEAVES - 1):
        q = 2 * p - LEAVES
        both = jnp.concatenate(
            [coef[:, q * 128 : (q + 1) * 128], coef[:, (q + 1) * 128 : (q + 2) * 128]], axis=0
        )
        value = diagonal(dot3(both, transfer[q : q + 2].reshape(128, 128), NT), vectors)
        coef[:, p * 128 : (p + 1) * 128] = value
    root = dot3(coef[:, 30 * 128 : 31 * 128], transfer[30], NT)
    root = jnp.concatenate([root, jnp.zeros((vectors, RANK), F32)], axis=1)
    coef[:, 31 * 128 :] = root
    for hbm in (up_hbm, down_hbm):
        out.append(start(coef.at[:, 2048:], hbm.at[vectors : 2 * vectors, 2048:]))
    for g in range(root_ref.shape[0]):
        root_ref[g] = root
    out.append(start(root_ref, root_hbm))
    for copy in out:
        copy.wait()


def source_tables(k, charges, points, select, sources, weights):
    parts = parts_of(points)
    sources[k] = dot(parts, select[:, 0:32], TN).astype(BF16)
    high, low = halves(charges)
    weights[k] = jnp.concatenate([high, low], axis=0)
    return parts


def empty_source(sources, weights):
    weights[LEAVES] = jnp.zeros(weights.shape[1:], BF16)
    sources[LEAVES] = sources[0]


def near_steps(list_ref, base, targets, tables, out_ref, highs, lows):
    sources, weights = tables
    vectors = out_ref.shape[0]

    def decode(j):
        code = list_ref[base + j]
        return lax.shift_right_logical(code, 8), jnp.bitwise_and(code, 255)

    def first(j, u, b):
        t, s = decode(j)
        high, low = halves(lax.rsqrt(dot(sources[s], targets[t])))
        highs[b][u][...] = high
        lows[b][u][...] = low

    def second(j, u, b):
        t, s = decode(j)
        q = weights[s]
        both = dot(q, highs[b][u][...])
        lanes = pl.ds(pl.multiple_of(t * PTS, PTS), PTS)
        out_ref[:, lanes] += both[:vectors] + both[vectors:] + dot(q[:vectors], lows[b][u][...])

    return first, second


def near_kernel(
    near_lists_hbm, far_hbm, charges_hbm, coords_hbm, select_hbm, select_t_hbm,
    near_hbm, targets_hbm, list_hbm, entry_hbm,
    near_lists, far_ref, far_vec, list_ref, entry_ref, coords, select, select_t, near_ref,
    charges, targets, *rest,
):
    tables, sems, tiles = rest[:2], rest[2], rest[3:]
    highs = (tiles[:LOCAL_GROUP], tiles[LOCAL_GROUP : 2 * LOCAL_GROUP])
    lows = (tiles[2 * LOCAL_GROUP : 3 * LOCAL_GROUP], tiles[3 * LOCAL_GROUP :])
    start = Copies(sems).start
    quarter = LEAVES // 4
    in_lists = [
        start(near_lists_hbm, near_lists),
        start(far_hbm, far_ref),
        start(far_hbm, far_vec),
    ]
    small = [start(coords_hbm, coords), start(select_hbm, select), start(select_t_hbm, select_t)]
    copies = []
    for i in range(4):
        lanes = slice(i * quarter * PTS, (i + 1) * quarter * PTS)
        copies.append(start(charges_hbm.at[:, lanes], charges.at[:, lanes]))
    near_ref[...] = jnp.zeros_like(near_ref)
    device = lax.axis_index(AXES)
    first = device * LEAVES
    for copy in in_lists:
        copy.wait()
    for q in range(QUADS):
        list_ref[STEPS + q] = q * 256 + 2 * q
    here, there, total = jnp.int32(0), jnp.int32(HALO), jnp.int32(STEPS + QUADS)
    entry = far_vec[...]
    entry_ref[:, 0:NODES] = jnp.where(entry >= 0, entry - (device - 1) * NODES, EMPTY)
    entry_ref[:, NODES:64] = jnp.full((SLOTS, 1), EMPTY, jnp.int32)
    for copy in small:
        copy.wait()
    for k in range(LEAVES):
        if k % quarter == 0:
            copies[k // quarter].wait()
        lanes = slice(k * PTS, (k + 1) * PTS)
        c = padded(scaled(coords[:, lanes]))
        parts = source_tables(k, charges[:, lanes], c, select, *tables)
        targets[k] = dot(select_t[...], parts).astype(BF16)
        for e in range(SLOTS):
            entry = near_lists[e, k]
            s = entry - first
            inside = jnp.logical_and(s >= 0, s < LEAVES)
            outside = jnp.logical_and(entry >= 0, jnp.logical_not(inside))
            list_ref[here] = k * 256 + s
            list_ref[there] = k * 256 + jnp.where(s < 0, s + REACH, s - REACH)
            here = here + inside.astype(jnp.int32)
            there = there + outside.astype(jnp.int32)
        if k < QUADS:
            columns = range(4 * k, min(4 * k + 4, NODES))
            tail = [far_ref[4 + e, c] for e in range(4) for c in columns]
            list_ref[total] = k * 256 + 2 * k + 1
            total = total + (functools.reduce(jnp.maximum, tail) >= 0).astype(jnp.int32)
    for u in range(PAD):
        list_ref[here + u] = LEAVES
        list_ref[there + u] = LEAVES
        list_ref[total + u] = QUADS * 256
    list_ref[COUNTS] = here
    list_ref[COUNTS + 1] = there - HALO
    list_ref[COUNTS + 2] = total - STEPS
    empty_source(*tables)
    outs = [
        start(targets, targets_hbm),
        start(list_ref, list_hbm),
        start(entry_ref, entry_hbm),
    ]
    stage = near_steps(list_ref, 0, targets, tables, near_ref, highs, lows)
    groups = (list_ref[COUNTS] + LOCAL_GROUP - 1) // LOCAL_GROUP
    pipelined(0, jnp.maximum(groups, 1) * LOCAL_GROUP, LOCAL_GROUP, [stage])
    outs.append(start(near_ref, near_hbm))
    for copy in outs:
        copy.wait()


def down_kernel(
    groups, list_hbm, entry_hbm,
    near_hbm, targets_hbm, lower_hbm, own_hbm, upper_hbm, basis_hbm, transfer_hbm,
    roots_hbm, skeleton_hbm, top_transfer_hbm, top_skeleton_hbm, select_hbm, select_t_hbm,
    out_hbm,
    list_ref, entry_ref, roots, skeleton, top_transfer, top_skeleton, select, select_t,
    near, near_local, targets, lower, own, upper, basis, transfer,
    sources, weights,
    nodes, pairs, feature, quads, coef_low, coef_high, local, top_coef,
    sems, *tiles,
):
    tables = (sources, weights)
    highs = (tiles[:GROUP], tiles[GROUP : 2 * GROUP])
    lows = (tiles[2 * GROUP : 3 * GROUP], tiles[3 * GROUP : 4 * GROUP])
    far_highs = (tiles[4 * GROUP : 5 * GROUP], tiles[5 * GROUP : 6 * GROUP])
    far_lows = (tiles[6 * GROUP : 7 * GROUP], tiles[7 * GROUP :])
    vectors = near.shape[0]
    device = lax.axis_index(AXES)
    low_mask = lower_lanes(vectors)
    coef_rows = slice(vectors, 2 * vectors)
    start = Copies(sems).start
    skeleton_in = [
        start(skeleton_hbm, skeleton),
        start(select_hbm, select),
        start(select_t_hbm, select_t),
    ]
    for copy in skeleton_in:
        copy.wait()
    halo_in = [
        start(roots_hbm, roots),
        start(top_transfer_hbm, top_transfer),
        start(top_skeleton_hbm, top_skeleton),
        start(list_hbm, list_ref),
        start(entry_hbm, entry_ref),
    ]
    for hbm, vmem in ((lower_hbm, lower), (upper_hbm, upper)):
        halo_in.append(start(hbm.at[0:vectors], vmem.at[0:vectors]))
        halo_in.append(start(hbm.at[2 * vectors :], vmem.at[2 * vectors :]))

    width = skeleton.shape[2]
    full = -(-width // 256) * 256
    raw = skeleton[...].reshape(3 * RANK, width)
    raw = jnp.concatenate([raw, jnp.zeros((3 * RANK, full - width), F32)], axis=1)
    shift = lax.rem(full - (device - 1) * NODES, full)
    window = pltpu.roll(raw, shift, 1)[:, :256]
    window = jnp.concatenate([scaled(window), jnp.zeros((RANK, 256), F32)], axis=0)
    window = window.T
    for i in range(2):
        nodes[i] = window[:, i * 128 : (i + 1) * 128]
    pairs[...] = jnp.zeros_like(pairs)
    for c in range(3):
        half = slice((c % 2) * RANK, (c % 2 + 1) * RANK)
        for base, first_node, count in ((0, 0, 96), (96, NODES, 32)):
            even = nodes[c // 2, pl.ds(first_node, count, stride=2), :][:, half]
            odd = nodes[c // 2, pl.ds(first_node + 1, count, stride=2), :][:, half]
            both = jnp.concatenate([even, odd], axis=1)
            pairs[pl.ds(base * 8 + c, count, stride=8), :] = both
    for g in range(24):
        c = jnp.concatenate([pairs[(4 * g + u) * 8 : (4 * g + u + 1) * 8] for u in range(4)], axis=1)
        value = dot(parts_of(c), select[...], TN).astype(BF16)
        feature[8 * g : 8 * g + 8] = value.reshape(8, RANK, 128)
    quad_lane = lax.broadcasted_iota(jnp.int32, (32, 256), 1) // RANK
    for q in range(QUADS):
        c = jnp.concatenate(
            [pairs[(96 + 2 * q + u) * 8 : (97 + 2 * q + u) * 8] for u in range(2)], axis=1
        )
        target = dot(select_t[...], parts_of(c))
        blocks = [jnp.where(quad_lane == i, target, 0.0) for i in range(4)]
        quads[q] = jnp.concatenate(blocks, axis=0).astype(BF16)

    for copy in halo_in:
        copy.wait()
    coef_in = [start(targets_hbm, targets)]
    for hbm, vmem in ((lower_hbm, lower), (own_hbm, own), (upper_hbm, upper)):
        coef_in.append(start(hbm.at[coef_rows], vmem.at[coef_rows]))
    bits = groups.bit_length() - 1
    offsets = []
    offset = 0
    for h in range(bits):
        count = groups >> h
        offsets.append(offset)
        for i in range(count // 2):
            if h == 0:
                pair = roots[2 * i] + pltpu.roll(roots[2 * i + 1], RANK, 1)
            else:
                row = groups - (groups >> (h - 1)) + 2 * i
                below = offsets[h - 1] + 2 * i
                both = top_coef[below : below + 2].reshape(2 * vectors, 128)
                matrix = top_transfer[row : row + 2].reshape(128, 128)
                pair = diagonal(dot3(both, matrix, NT), vectors)
            top_coef[offset + i] = pair
        offset += count // 2
    upper_row = lax.broadcasted_iota(jnp.int32, (128, 128), 0) < RANK
    upper_lane = lax.broadcasted_iota(jnp.int32, (128, 128), 1) < RANK
    couple = []
    for h in range(bits):
        node = device // 2**h
        i = node // 2
        if h == 0:
            rows = [
                jnp.concatenate(
                    [nodes[c // 2, r : r + 1, c % 2 * RANK : (c % 2 + 1) * RANK] for c in range(3)],
                    axis=0,
                )
                for r in (NODES - 1, 2 * NODES - 1, 3 * NODES - 1)
            ]
            odd = node % 2 == 1
            left = jnp.where(odd, rows[0], rows[1])
            right = jnp.where(odd, rows[1], rows[2])
        else:
            row = groups - (groups >> (h - 1))
            left = scaled(top_skeleton[row + 2 * i])
            right = scaled(top_skeleton[row + 2 * i + 1])
        parts = parts_of(padded(jnp.concatenate([left, right], axis=1)))
        source = dot(parts, select[:, 0:32], TN).astype(BF16)
        target = dot(select_t[...], parts).astype(BF16)
        tile = jnp.where(upper_row != upper_lane, lax.rsqrt(dot(source, target)), 0.0)
        couple.append(dot3(top_coef[offsets[h] + i], tile))
    top = couple[bits - 1]
    for h in range(bits - 2, -1, -1):
        parent = device // 2 ** (h + 1)
        mine = jnp.where(low_mask == (parent % 2 == 0), top, 0.0)
        row = groups - (groups >> h) + 2 * (parent // 2)
        matrix = top_transfer[pl.ds(row, 2)].reshape(128, 128)
        top = couple[h] + dot3(mine, matrix)
    top = jnp.where(device % 2 == 1, pltpu.roll(top, RANK, 1), top)

    for k in range(LEAVES):
        buffer = lower if k < REACH else upper
        lanes = slice((k % REACH) * PTS, (k % REACH + 1) * PTS)
        c = padded(scaled(buffer[2 * vectors : 2 * vectors + 3, lanes]))
        source_tables(k, buffer[0:vectors, lanes], c, select, *tables)
    empty_source(*tables)
    for copy in coef_in:
        copy.wait()
    late_in = [start(transfer_hbm, transfer), start(basis_hbm, basis), start(near_hbm, near_local)]
    near[...] = jnp.zeros_like(near)
    for b, buffer in enumerate((lower, own, upper)):
        for p in range(32):
            pair = buffer[coef_rows, p * 128 : (p + 1) * 128]
            swap = pltpu.roll(pair, RANK, 1)
            zero = jnp.zeros_like(pair)
            for n, (a, c) in enumerate(((pair, swap), (swap, pair))):
                if 2 * p + n == NODES:
                    continue
                for table, value in (
                    (coef_low, jnp.where(low_mask, a, zero)),
                    (coef_high, jnp.where(low_mask, zero, c)),
                ):
                    high, low = halves(value)
                    table[b * NODES + 2 * p + n] = jnp.concatenate([high, low], axis=0)
    coef_low[EMPTY] = jnp.zeros((2 * vectors, 128), BF16)
    coef_high[EMPTY] = jnp.zeros((2 * vectors, 128), BF16)
    local[...] = jnp.zeros_like(local)
    lane_group = lax.broadcasted_iota(jnp.int32, (RANK, 128), 1) // 32

    def entries(j):
        code = list_ref[STEPS + j]
        target = lax.shift_right_logical(code, 8)
        chunk = jnp.bitwise_and(code, 255)
        q = lax.shift_right_logical(chunk, 1)
        slot = 4 * jnp.bitwise_and(chunk, 1)
        return target, q, [[entry_ref[slot + e, 4 * q + i] for e in range(4)] for i in range(4)]

    def far_first(j, u, b):
        target, q, picks = entries(j)
        rows = []
        for e in range(4):
            value = feature[picks[3][e]]
            for i in range(3):
                value = jnp.where(lane_group == i, feature[picks[i][e]], value)
            rows.append(value)
        high, low = halves(lax.rsqrt(dot(jnp.concatenate(rows, axis=0), quads[q])))
        far_highs[b][u][...] = high
        far_lows[b][u][...] = low

    def far_second(j, u, b):
        target, q, picks = entries(j)
        sides = []
        for s in picks:
            left = coef_low[s[0]] + coef_high[s[1]]
            right = coef_low[s[2]] + coef_high[s[3]]
            sides.append(jnp.concatenate([left, right], axis=1))
        for p in range(2):
            pair = sides[2 * p : 2 * p + 2]
            high = [side[:vectors] for side in pair]
            low = [side[vectors:] for side in pair]
            lanes = slice(p * 128, (p + 1) * 128)
            both = dot(jnp.concatenate(high + low, axis=0), far_highs[b][u][:, lanes])
            rest = dot(jnp.concatenate(high, axis=0), far_lows[b][u][:, lanes])
            value = both[: 2 * vectors] + both[2 * vectors :] + rest
            local[2 * target + p] += diagonal(value, vectors)

    near_stage = near_steps(list_ref, HALO, targets, tables, near, highs, lows)
    far_stage = (far_first, far_second)
    near_end = (list_ref[COUNTS + 1] + GROUP - 1) // GROUP * GROUP
    far_end = (list_ref[COUNTS + 2] + GROUP - 1) // GROUP * GROUP
    shared = jnp.minimum(near_end, far_end)

    @pl.when(shared > 0)
    def _():
        pipelined(0, shared, GROUP, [near_stage, far_stage])

    @pl.when(near_end > shared)
    def _():
        pipelined(shared, near_end, GROUP, [near_stage])

    @pl.when(far_end > shared)
    def _():
        pipelined(shared, far_end, GROUP, [far_stage])


    for copy in late_in:
        copy.wait()
    local[30] += dot3(jnp.where(low_mask, local[31] + top, 0.0)[:, :RANK], transfer[30])
    for p in range(30, 15, -1):
        q = 2 * p - LEAVES
        both = dot3(spread_pair(local[p]), transfer[q : q + 2].reshape(128, 128))
        local[q] += both[:vectors]
        local[q + 1] += both[vectors:]
    out = []
    for p in range(LEAVES // 2):
        both = dot3(spread_pair(local[p]), basis[2 * p : 2 * p + 2].reshape(128, PTS))
        for c in range(2):
            lanes = slice((2 * p + c) * PTS, (2 * p + c + 1) * PTS)
            close = near[:, lanes] + near_local[:, lanes]
            near[:, lanes] = both[c * vectors : (c + 1) * vectors] + NEAR_WEIGHT * close
        if p % 4 == 3:
            lanes = slice((p - 3) * 2 * PTS, (p + 1) * 2 * PTS)
            out.append(start(near.at[:, lanes], out_hbm.at[:, lanes]))
    for copy in out:
        copy.wait()


def whole(count, space=pltpu.VMEM):
    return [pl.BlockSpec(memory_space=space)] * count


def on_device(
    charges, coordinates, near_lists, far_lists, leaf_basis, local_transfer,
    skeleton, top_transfer, top_skeleton,
):
    vectors = charges.shape[0]
    groups = lax.axis_size(AXES)
    points = LEAVES * PTS
    height = 2 * vectors + ROWS
    shape = jax.ShapeDtypeStruct
    select, select_t = selections()
    params = pltpu.CompilerParams(vmem_limit_bytes=(64 << 20) - (64 << 10))
    smem = pltpu.SMEM
    vmem = pltpu.VMEM
    matrices = [vmem((LEAVES, RANK, PTS), F32), vmem((LEAVES - 1, RANK, 128), F32)]
    list_shape = (LISTS,)
    up, down, root = pl.pallas_call(
        up_kernel,
        out_shape=[
            shape((height, HALF), F32),
            shape((height, HALF), F32),
            shape((groups, vectors, 128), F32),
        ],
        in_specs=whole(4, pl.ANY),
        out_specs=whole(3, pl.ANY),
        scratch_shapes=[
            vmem((3, points), F32),
            vmem((groups, vectors, 128), F32),
            vmem((vectors, points), F32),
            vmem((ROWS, points), F32),
        ]
        + matrices
        + [vmem((vectors, 32 * 128), F32), pltpu.SemaphoreType.DMA((24,))],
        compiler_params=params,
    )(charges, coordinates, leaf_basis, local_transfer)

    upward = [(i, i + 1) for i in range(groups - 1)]
    lower = lax.ppermute(up, AXES, upward)
    upper = lax.ppermute(down, AXES, [(j, i) for i, j in upward])
    roots = lax.all_to_all(root, AXES, 0, 0)

    tile = vmem((PTS, PTS), BF16)
    tables = [
        vmem((LEAVES + 1, PTS, 32), BF16),
        vmem((LEAVES + 1, 2 * vectors, PTS), BF16),
    ]
    selects = [vmem(select.shape, BF16), vmem(select_t.shape, BF16)]
    near, targets, lists, entries = pl.pallas_call(
        near_kernel,
        out_shape=[
            shape((vectors, points), F32),
            shape((LEAVES, 32, PTS), BF16),
            shape(list_shape, jnp.int32),
            shape((SLOTS, 64), jnp.int32),
        ],
        in_specs=whole(6, pl.ANY),
        out_specs=whole(4, pl.ANY),
        scratch_shapes=[
            smem((SLOTS, LEAVES), jnp.int32),
            smem((SLOTS, NODES), jnp.int32),
            vmem((SLOTS, NODES), jnp.int32),
            smem(list_shape, jnp.int32),
            vmem((SLOTS, 64), jnp.int32),
            vmem((3, points), F32),
        ]
        + selects
        + [vmem((vectors, points), F32)] * 2
        + [vmem((LEAVES, 32, PTS), BF16)]
        + tables
        + [pltpu.SemaphoreType.DMA((16,))]
        + [tile] * (4 * LOCAL_GROUP),
        compiler_params=params,
        cost_estimate=pl.CostEstimate(
            flops=192 * 3 * 2 * PTS**3, transcendentals=192 * PTS**2, bytes_accessed=4 << 20
        ),
    )(near_lists.T, far_lists.T, charges, coordinates, select, select_t)

    skeletons = skeleton.transpose(1, 2, 0)
    return pl.pallas_call(
        functools.partial(down_kernel, groups),
        out_shape=shape((vectors, points), F32),
        in_specs=whole(15, pl.ANY),
        out_specs=pl.BlockSpec(memory_space=pl.ANY),
        scratch_shapes=[
            smem(list_shape, jnp.int32),
            smem((SLOTS, 64), jnp.int32),
            vmem((groups, vectors, 128), F32),
            vmem(skeletons.shape, F32),
            vmem(top_transfer.shape, F32),
            vmem(top_skeleton.shape, F32),
        ]
        + selects
        + [vmem((vectors, points), F32)] * 2
        + [vmem((LEAVES, 32, PTS), BF16)]
        + [vmem((height, HALF), F32)] * 3
        + matrices
        + tables
        + [
            vmem((2, 256, 128), F32),
            vmem((128 * 8, 128), F32),
            vmem((192, RANK, 128), BF16),
            vmem((QUADS, 128, 256), BF16),
            vmem((EMPTY + 1, 2 * vectors, 128), BF16),
            vmem((EMPTY + 1, 2 * vectors, 128), BF16),
            vmem((2 * QUADS + 2, vectors, 128), F32),
            vmem((groups, vectors, 128), F32),
            pltpu.SemaphoreType.DMA((24,)),
        ]
        + [tile] * (8 * GROUP),
        compiler_params=params,
    )(
        lists, entries, near, targets, lower, up, upper, leaf_basis, local_transfer,
        roots, skeletons, top_transfer, top_skeleton, select, select_t,
    )


def solution(mesh):
    placed = (
        P("vec", ("parts", "leaf", "sub")),
        P(None, ("parts", "leaf", "sub")),
        P(("parts", "leaf", "sub"), None),
        P(("parts", "leaf", "sub"), None),
        P(("parts", "leaf", "sub"), None, None),
        P(("parts", "leaf", "sub"), None, None),
        P("parts", None, None),
        P("parts", None, None),
        P("parts", None, None),
    )
    return jax.shard_map(
        on_device,
        mesh=mesh,
        in_specs=placed,
        out_specs=P("vec", ("parts", "leaf", "sub")),
        check_vma=False,
    )
```

```python
import functools

import jax
import jax.numpy as jnp
import numpy as np
from jax import lax
from jax.experimental import pallas as pl
from jax.experimental.pallas import tpu as pltpu
from jax.sharding import PartitionSpec as P

PTS = 256
RANK = 64
LEAVES = 32
NODES = 63
SLOTS = 8
REACH = 16
HALF = REACH * PTS
ROWS = 8
PAD = 16
HALO = LEAVES * SLOTS + PAD
STEPS = 2 * HALO
COUNTS = STEPS + 48
LISTS = COUNTS + 16
LOCAL_GROUP = 6
GROUP = 4
WIDTH = 0.05
NEAR_WEIGHT = 0.0625
EMPTY = 3 * NODES
QUADS = 16
F32 = jnp.float32
BF16 = jnp.bfloat16
AXES = ("leaf", "sub")
NN = (((1,), (0,)), ((), ()))
NT = (((1,), (1,)), ((), ()))
TN = (((0,), (0,)), ((), ()))


def selections():
    source_part = (1, 1, 2, 2, 1, 3)
    target_part = (1, 2, 1, 2, 3, 1)
    source = np.zeros((64, 32), np.float32)
    target = np.zeros((32, 64), np.float32)
    for g in range(6):
        for c in range(3):
            source[(source_part[g] - 1) * 8 + c, 4 * g + c] = 1
            target[4 * g + c, (target_part[g] - 1) * 8 + c] = -2
        f = 4 * g + 3
        if g < 3:
            source[24 + 8 * g, f] = 1
            target[f, 48] = 1
        else:
            source[48, f] = 1
            target[f, 24 + 8 * (g - 3)] = 1
    source[48, 24] = 1
    target[24, 48] = 1
    return jnp.asarray(np.tile(source, (1, 4)), BF16), jnp.asarray(target, BF16)


def halves(x):
    high = x.astype(BF16)
    return high, (x - high.astype(F32)).astype(BF16)


def dot(a, b, dims=NN):
    return lax.dot_general(a, b, dims, preferred_element_type=F32)


def dot3(a, b, dims=NN):
    ah, al = halves(a)
    bh, bl = halves(b)
    rows = a.shape[0]
    both = dot(jnp.concatenate([ah, al], axis=0), bh, dims)
    return both[:rows] + both[rows:] + dot(ah, bl, dims)


def scaled(points):
    return (points - 0.5) * (1.0 / WIDTH)


def padded(points):
    return jnp.concatenate([points, jnp.zeros((5, points.shape[1]), F32)], axis=0)


def parts_of(c):
    n = c.shape[1]

    def rounded(x):
        return x.astype(BF16).astype(F32)

    p1 = rounded(c)
    rest = c - p1
    p2 = rounded(rest)
    p3 = rest - p2
    norm = jnp.broadcast_to(jnp.sum(c * c, axis=0, keepdims=True), (8, n))
    n1 = rounded(norm)
    rest = norm - n1
    n2 = rounded(rest)
    n3 = rest - n2
    rows = [p1, p2, p3, n1, n2, n3, jnp.ones((8, n), F32), jnp.zeros((8, n), F32)]
    return jnp.concatenate(rows, axis=0).astype(BF16)


def lower_lanes(rows):
    return lax.broadcasted_iota(jnp.int32, (rows, 128), 1) < RANK


def diagonal(x, vectors):
    return jnp.where(lower_lanes(vectors), x[:vectors], x[vectors:])


def spread_pair(pair):
    low = lower_lanes(pair.shape[0])
    zero = jnp.zeros_like(pair)
    return jnp.concatenate([jnp.where(low, pair, zero), jnp.where(low, zero, pair)], axis=0)


def pipelined(begin, end, group, stages):
    def first(base, h):
        for u in range(group):
            for stage in stages:
                stage[0](base + u, u, h)

    def second(base, h):
        for u in range(group):
            for stage in stages:
                stage[1](base + u, u, h)

    def both(base, h):
        first(base + group, 1 - h)
        second(base, h)

    first(begin, 0)
    more = (end - begin) // group - 1

    def body(i, carry):
        base = begin + 2 * i * group
        both(base, 0)
        both(base + group, 1)
        return carry

    lax.fori_loop(0, more // 2, body, 0)
    base = begin + more // 2 * 2 * group

    @pl.when(more % 2 == 1)
    def _():
        both(base, 0)
        second(base + group, 1)

    @pl.when(more % 2 == 0)
    def _():
        second(base, 0)


class Copies:
    def __init__(self, sems):
        self.sems = sems
        self.count = 0

    def start(self, source, target):
        copy = pltpu.make_async_copy(source, target, self.sems.at[self.count])
        self.count += 1
        copy.start()
        return copy


def up_kernel(
    charges_hbm, coords_hbm, basis_hbm, transfer_hbm,
    up_hbm, down_hbm, root_hbm,
    coords, root_ref,
    charges, points, basis, transfer, coef, sems,
):
    vectors = charges.shape[0]
    start = Copies(sems).start
    quarter = LEAVES // 4
    in_coords = start(coords_hbm, coords)
    incoming = []

    def fetch(i):
        lanes = slice(i * quarter * PTS, (i + 1) * quarter * PTS)
        leaves = slice(i * quarter, (i + 1) * quarter)
        incoming.append(start(charges_hbm.at[:, lanes], charges.at[:, lanes]))
        incoming.append(start(basis_hbm.at[leaves], basis.at[leaves]))

    for i in range(4):
        fetch(i)
    in_transfer = start(transfer_hbm, transfer)
    in_coords.wait()
    points[0:3] = coords[...]
    points[3:] = jnp.zeros((ROWS - 3, points.shape[1]), F32)

    out = [
        start(points.at[:, HALF:], up_hbm.at[2 * vectors :]),
        start(points.at[:, :HALF], down_hbm.at[2 * vectors :]),
    ]
    per = LEAVES // 8
    for p in range(LEAVES // 2):
        if p % per == 0:
            i = p // per
            incoming[2 * i].wait()
            incoming[2 * i + 1].wait()
            if p == per:
                out.append(start(charges.at[:, :HALF], down_hbm.at[0:vectors]))
            if p == 3 * per:
                out.append(start(charges.at[:, HALF:], up_hbm.at[0:vectors]))
        a, b = slice(2 * p * PTS, (2 * p + 1) * PTS), slice((2 * p + 1) * PTS, (2 * p + 2) * PTS)
        both = jnp.concatenate([charges[:, a], charges[:, b]], axis=0)
        value = diagonal(dot3(both, basis[2 * p : 2 * p + 2].reshape(2 * RANK, PTS), NT), vectors)
        coef[:, p * 128 : (p + 1) * 128] = value
    for hbm in (up_hbm, down_hbm):
        out.append(start(coef.at[:, :2048], hbm.at[vectors : 2 * vectors, :2048]))
    in_transfer.wait()
    for p in range(LEAVES // 2, LEAVES - 1):
        q = 2 * p - LEAVES
        both = jnp.concatenate(
            [coef[:, q * 128 : (q + 1) * 128], coef[:, (q + 1) * 128 : (q + 2) * 128]], axis=0
        )
        value = diagonal(dot3(both, transfer[q : q + 2].reshape(128, 128), NT), vectors)
        coef[:, p * 128 : (p + 1) * 128] = value
    root = dot3(coef[:, 30 * 128 : 31 * 128], transfer[30], NT)
    root = jnp.concatenate([root, jnp.zeros((vectors, RANK), F32)], axis=1)
    coef[:, 31 * 128 :] = root
    for hbm in (up_hbm, down_hbm):
        out.append(start(coef.at[:, 2048:], hbm.at[vectors : 2 * vectors, 2048:]))
    for g in range(root_ref.shape[0]):
        root_ref[g] = root
    out.append(start(root_ref, root_hbm))
    for copy in out:
        copy.wait()


def source_tables(k, charges, points, select, sources, weights):
    parts = parts_of(points)
    sources[k] = dot(parts, select[:, 0:32], TN).astype(BF16)
    high, low = halves(charges)
    weights[k] = jnp.concatenate([high, low], axis=0)
    return parts


def empty_source(sources, weights):
    weights[LEAVES] = jnp.zeros(weights.shape[1:], BF16)
    sources[LEAVES] = sources[0]


def near_steps(list_ref, base, targets, tables, out_ref, highs, lows):
    sources, weights = tables
    vectors = out_ref.shape[0]

    def decode(j):
        code = list_ref[base + j]
        return lax.shift_right_logical(code, 8), jnp.bitwise_and(code, 255)

    def first(j, u, b):
        t, s = decode(j)
        high, low = halves(lax.rsqrt(dot(sources[s], targets[t])))
        highs[b][u][...] = high
        lows[b][u][...] = low

    def second(j, u, b):
        t, s = decode(j)
        q = weights[s]
        both = dot(q, highs[b][u][...])
        lanes = pl.ds(pl.multiple_of(t * PTS, PTS), PTS)
        out_ref[:, lanes] += both[:vectors] + both[vectors:] + dot(q[:vectors], lows[b][u][...])

    return first, second


def near_kernel(
    near_lists_hbm, far_hbm, charges_hbm, coords_hbm, select_hbm, select_t_hbm,
    near_hbm, targets_hbm, list_hbm, entry_hbm,
    near_lists, far_ref, far_vec, list_ref, entry_ref, coords, select, select_t, near_ref,
    charges, targets, *rest,
):
    tables, sems, tiles = rest[:2], rest[2], rest[3:]
    highs = (tiles[:LOCAL_GROUP], tiles[LOCAL_GROUP : 2 * LOCAL_GROUP])
    lows = (tiles[2 * LOCAL_GROUP : 3 * LOCAL_GROUP], tiles[3 * LOCAL_GROUP :])
    start = Copies(sems).start
    quarter = LEAVES // 4
    in_lists = [
        start(near_lists_hbm, near_lists),
        start(far_hbm, far_ref),
        start(far_hbm, far_vec),
    ]
    small = [start(coords_hbm, coords), start(select_hbm, select), start(select_t_hbm, select_t)]
    copies = []
    for i in range(4):
        lanes = slice(i * quarter * PTS, (i + 1) * quarter * PTS)
        copies.append(start(charges_hbm.at[:, lanes], charges.at[:, lanes]))
    near_ref[...] = jnp.zeros_like(near_ref)
    device = lax.axis_index(AXES)
    first = device * LEAVES
    for copy in in_lists:
        copy.wait()
    for q in range(QUADS):
        list_ref[STEPS + q] = q * 256 + 2 * q
    here, there, total = jnp.int32(0), jnp.int32(HALO), jnp.int32(STEPS + QUADS)
    entry = far_vec[...]
    entry_ref[:, 0:NODES] = jnp.where(entry >= 0, entry - (device - 1) * NODES, EMPTY)
    entry_ref[:, NODES:64] = jnp.full((SLOTS, 1), EMPTY, jnp.int32)
    for copy in small:
        copy.wait()
    for k in range(LEAVES):
        if k % quarter == 0:
            copies[k // quarter].wait()
        lanes = slice(k * PTS, (k + 1) * PTS)
        c = padded(scaled(coords[:, lanes]))
        parts = source_tables(k, charges[:, lanes], c, select, *tables)
        targets[k] = dot(select_t[...], parts).astype(BF16)
        for e in range(SLOTS):
            entry = near_lists[e, k]
            s = entry - first
            inside = jnp.logical_and(s >= 0, s < LEAVES)
            outside = jnp.logical_and(entry >= 0, jnp.logical_not(inside))
            list_ref[here] = k * 256 + s
            list_ref[there] = k * 256 + jnp.where(s < 0, s + REACH, s - REACH)
            here = here + inside.astype(jnp.int32)
            there = there + outside.astype(jnp.int32)
        if k < QUADS:
            columns = range(4 * k, min(4 * k + 4, NODES))
            tail = [far_ref[4 + e, c] for e in range(4) for c in columns]
            list_ref[total] = k * 256 + 2 * k + 1
            total = total + (functools.reduce(jnp.maximum, tail) >= 0).astype(jnp.int32)
    for u in range(PAD):
        list_ref[here + u] = LEAVES
        list_ref[there + u] = LEAVES
        list_ref[total + u] = QUADS * 256
    list_ref[COUNTS] = here
    list_ref[COUNTS + 1] = there - HALO
    list_ref[COUNTS + 2] = total - STEPS
    empty_source(*tables)
    outs = [
        start(targets, targets_hbm),
        start(list_ref, list_hbm),
        start(entry_ref, entry_hbm),
    ]
    stage = near_steps(list_ref, 0, targets, tables, near_ref, highs, lows)
    groups = (list_ref[COUNTS] + LOCAL_GROUP - 1) // LOCAL_GROUP
    pipelined(0, jnp.maximum(groups, 1) * LOCAL_GROUP, LOCAL_GROUP, [stage])
    outs.append(start(near_ref, near_hbm))
    for copy in outs:
        copy.wait()


def down_kernel(
    groups, list_hbm, entry_hbm,
    near_hbm, targets_hbm, lower_hbm, own_hbm, upper_hbm, basis_hbm, transfer_hbm,
    roots_hbm, skeleton_hbm, top_transfer_hbm, top_skeleton_hbm, select_hbm, select_t_hbm,
    out_hbm,
    list_ref, entry_ref, roots, skeleton, top_transfer, top_skeleton, select, select_t,
    near, near_local, targets, lower, own, upper, basis, transfer,
    sources, weights,
    nodes, pairs, feature, quads, coef_low, coef_high, local, top_coef,
    sems, *tiles,
):
    tables = (sources, weights)
    highs = (tiles[:GROUP], tiles[GROUP : 2 * GROUP])
    lows = (tiles[2 * GROUP : 3 * GROUP], tiles[3 * GROUP : 4 * GROUP])
    far_highs = (tiles[4 * GROUP : 5 * GROUP], tiles[5 * GROUP : 6 * GROUP])
    far_lows = (tiles[6 * GROUP : 7 * GROUP], tiles[7 * GROUP :])
    vectors = near.shape[0]
    device = lax.axis_index(AXES)
    low_mask = lower_lanes(vectors)
    coef_rows = slice(vectors, 2 * vectors)
    start = Copies(sems).start
    skeleton_in = [
        start(skeleton_hbm, skeleton),
        start(select_hbm, select),
        start(select_t_hbm, select_t),
    ]
    for copy in skeleton_in:
        copy.wait()
    halo_in = [
        start(roots_hbm, roots),
        start(top_transfer_hbm, top_transfer),
        start(top_skeleton_hbm, top_skeleton),
        start(list_hbm, list_ref),
        start(entry_hbm, entry_ref),
    ]
    for hbm, vmem in ((lower_hbm, lower), (upper_hbm, upper)):
        halo_in.append(start(hbm.at[0:vectors], vmem.at[0:vectors]))
        halo_in.append(start(hbm.at[2 * vectors :], vmem.at[2 * vectors :]))

    width = skeleton.shape[2]
    full = -(-width // 256) * 256
    raw = skeleton[...].reshape(3 * RANK, width)
    raw = jnp.concatenate([raw, jnp.zeros((3 * RANK, full - width), F32)], axis=1)
    shift = lax.rem(full - (device - 1) * NODES, full)
    window = pltpu.roll(raw, shift, 1)[:, :256]
    window = jnp.concatenate([scaled(window), jnp.zeros((RANK, 256), F32)], axis=0)
    window = window.T
    for i in range(2):
        nodes[i] = window[:, i * 128 : (i + 1) * 128]
    pairs[...] = jnp.zeros_like(pairs)
    for c in range(3):
        half = slice((c % 2) * RANK, (c % 2 + 1) * RANK)
        for base, first_node, count in ((0, 0, 96), (96, NODES, 32)):
            even = nodes[c // 2, pl.ds(first_node, count, stride=2), :][:, half]
            odd = nodes[c // 2, pl.ds(first_node + 1, count, stride=2), :][:, half]
            both = jnp.concatenate([even, odd], axis=1)
            pairs[pl.ds(base * 8 + c, count, stride=8), :] = both
    for g in range(24):
        c = jnp.concatenate([pairs[(4 * g + u) * 8 : (4 * g + u + 1) * 8] for u in range(4)], axis=1)
        value = dot(parts_of(c), select[...], TN).astype(BF16)
        feature[8 * g : 8 * g + 8] = value.reshape(8, RANK, 128)
    quad_lane = lax.broadcasted_iota(jnp.int32, (32, 256), 1) // RANK
    for q in range(QUADS):
        c = jnp.concatenate(
            [pairs[(96 + 2 * q + u) * 8 : (97 + 2 * q + u) * 8] for u in range(2)], axis=1
        )
        target = dot(select_t[...], parts_of(c))
        blocks = [jnp.where(quad_lane == i, target, 0.0) for i in range(4)]
        quads[q] = jnp.concatenate(blocks, axis=0).astype(BF16)

    for copy in halo_in:
        copy.wait()
    coef_in = [start(targets_hbm, targets)]
    for hbm, vmem in ((lower_hbm, lower), (own_hbm, own), (upper_hbm, upper)):
        coef_in.append(start(hbm.at[coef_rows], vmem.at[coef_rows]))
    bits = groups.bit_length() - 1
    offsets = []
    offset = 0
    for h in range(bits):
        count = groups >> h
        offsets.append(offset)
        for i in range(count // 2):
            if h == 0:
                pair = roots[2 * i] + pltpu.roll(roots[2 * i + 1], RANK, 1)
            else:
                row = groups - (groups >> (h - 1)) + 2 * i
                below = offsets[h - 1] + 2 * i
                both = top_coef[below : below + 2].reshape(2 * vectors, 128)
                matrix = top_transfer[row : row + 2].reshape(128, 128)
                pair = diagonal(dot3(both, matrix, NT), vectors)
            top_coef[offset + i] = pair
        offset += count // 2
    upper_row = lax.broadcasted_iota(jnp.int32, (128, 128), 0) < RANK
    upper_lane = lax.broadcasted_iota(jnp.int32, (128, 128), 1) < RANK
    couple = []
    for h in range(bits):
        node = device // 2**h
        i = node // 2
        if h == 0:
            rows = [
                jnp.concatenate(
                    [nodes[c // 2, r : r + 1, c % 2 * RANK : (c % 2 + 1) * RANK] for c in range(3)],
                    axis=0,
                )
                for r in (NODES - 1, 2 * NODES - 1, 3 * NODES - 1)
            ]
            odd = node % 2 == 1
            left = jnp.where(odd, rows[0], rows[1])
            right = jnp.where(odd, rows[1], rows[2])
        else:
            row = groups - (groups >> (h - 1))
            left = scaled(top_skeleton[row + 2 * i])
            right = scaled(top_skeleton[row + 2 * i + 1])
        parts = parts_of(padded(jnp.concatenate([left, right], axis=1)))
        source = dot(parts, select[:, 0:32], TN).astype(BF16)
        target = dot(select_t[...], parts).astype(BF16)
        tile = jnp.where(upper_row != upper_lane, lax.rsqrt(dot(source, target)), 0.0)
        couple.append(dot3(top_coef[offsets[h] + i], tile))
    top = couple[bits - 1]
    for h in range(bits - 2, -1, -1):
        parent = device // 2 ** (h + 1)
        mine = jnp.where(low_mask == (parent % 2 == 0), top, 0.0)
        row = groups - (groups >> h) + 2 * (parent // 2)
        matrix = top_transfer[pl.ds(row, 2)].reshape(128, 128)
        top = couple[h] + dot3(mine, matrix)
    top = jnp.where(device % 2 == 1, pltpu.roll(top, RANK, 1), top)

    for k in range(LEAVES):
        buffer = lower if k < REACH else upper
        lanes = slice((k % REACH) * PTS, (k % REACH + 1) * PTS)
        c = padded(scaled(buffer[2 * vectors : 2 * vectors + 3, lanes]))
        source_tables(k, buffer[0:vectors, lanes], c, select, *tables)
    empty_source(*tables)
    for copy in coef_in:
        copy.wait()
    late_in = [start(transfer_hbm, transfer), start(basis_hbm, basis), start(near_hbm, near_local)]
    near[...] = jnp.zeros_like(near)
    for b, buffer in enumerate((lower, own, upper)):
        for p in range(32):
            pair = buffer[coef_rows, p * 128 : (p + 1) * 128]
            swap = pltpu.roll(pair, RANK, 1)
            zero = jnp.zeros_like(pair)
            for n, (a, c) in enumerate(((pair, swap), (swap, pair))):
                if 2 * p + n == NODES:
                    continue
                for table, value in (
                    (coef_low, jnp.where(low_mask, a, zero)),
                    (coef_high, jnp.where(low_mask, zero, c)),
                ):
                    high, low = halves(value)
                    table[b * NODES + 2 * p + n] = jnp.concatenate([high, low], axis=0)
    coef_low[EMPTY] = jnp.zeros((2 * vectors, 128), BF16)
    coef_high[EMPTY] = jnp.zeros((2 * vectors, 128), BF16)
    local[...] = jnp.zeros_like(local)
    lane_group = lax.broadcasted_iota(jnp.int32, (RANK, 128), 1) // 32

    def entries(j):
        code = list_ref[STEPS + j]
        target = lax.shift_right_logical(code, 8)
        chunk = jnp.bitwise_and(code, 255)
        q = lax.shift_right_logical(chunk, 1)
        slot = 4 * jnp.bitwise_and(chunk, 1)
        return target, q, [[entry_ref[slot + e, 4 * q + i] for e in range(4)] for i in range(4)]

    def far_first(j, u, b):
        target, q, picks = entries(j)
        rows = []
        for e in range(4):
            value = feature[picks[3][e]]
            for i in range(3):
                value = jnp.where(lane_group == i, feature[picks[i][e]], value)
            rows.append(value)
        high, low = halves(lax.rsqrt(dot(jnp.concatenate(rows, axis=0), quads[q])))
        far_highs[b][u][...] = high
        far_lows[b][u][...] = low

    def far_second(j, u, b):
        target, q, picks = entries(j)
        sides = []
        for s in picks:
            left = coef_low[s[0]] + coef_high[s[1]]
            right = coef_low[s[2]] + coef_high[s[3]]
            sides.append(jnp.concatenate([left, right], axis=1))
        for p in range(2):
            pair = sides[2 * p : 2 * p + 2]
            high = [side[:vectors] for side in pair]
            low = [side[vectors:] for side in pair]
            lanes = slice(p * 128, (p + 1) * 128)
            both = dot(jnp.concatenate(high + low, axis=0), far_highs[b][u][:, lanes])
            rest = dot(jnp.concatenate(high, axis=0), far_lows[b][u][:, lanes])
            value = both[: 2 * vectors] + both[2 * vectors :] + rest
            local[2 * target + p] += diagonal(value, vectors)

    near_stage = near_steps(list_ref, HALO, targets, tables, near, highs, lows)
    far_stage = (far_first, far_second)
    near_end = (list_ref[COUNTS + 1] + GROUP - 1) // GROUP * GROUP
    far_end = (list_ref[COUNTS + 2] + GROUP - 1) // GROUP * GROUP
    shared = jnp.minimum(near_end, far_end)

    @pl.when(shared > 0)
    def _():
        pipelined(0, shared, GROUP, [near_stage, far_stage])

    @pl.when(near_end > shared)
    def _():
        pipelined(shared, near_end, GROUP, [near_stage])

    @pl.when(far_end > shared)
    def _():
        pipelined(shared, far_end, GROUP, [far_stage])


    for copy in late_in:
        copy.wait()
    local[30] += dot3(jnp.where(low_mask, local[31] + top, 0.0)[:, :RANK], transfer[30])
    for p in range(30, 15, -1):
        q = 2 * p - LEAVES
        both = dot3(spread_pair(local[p]), transfer[q : q + 2].reshape(128, 128))
        local[q] += both[:vectors]
        local[q + 1] += both[vectors:]
    out = []
    for p in range(LEAVES // 2):
        both = dot3(spread_pair(local[p]), basis[2 * p : 2 * p + 2].reshape(128, PTS))
        for c in range(2):
            lanes = slice((2 * p + c) * PTS, (2 * p + c + 1) * PTS)
            close = near[:, lanes] + near_local[:, lanes]
            near[:, lanes] = both[c * vectors : (c + 1) * vectors] + NEAR_WEIGHT * close
        if p % 4 == 3:
            lanes = slice((p - 3) * 2 * PTS, (p + 1) * 2 * PTS)
            out.append(start(near.at[:, lanes], out_hbm.at[:, lanes]))
    for copy in out:
        copy.wait()


def whole(count, space=pltpu.VMEM):
    return [pl.BlockSpec(memory_space=space)] * count


def on_device(
    charges, coordinates, near_lists, far_lists, leaf_basis, local_transfer,
    skeleton, top_transfer, top_skeleton,
):
    vectors = charges.shape[0]
    groups = lax.axis_size(AXES)
    points = LEAVES * PTS
    height = 2 * vectors + ROWS
    shape = jax.ShapeDtypeStruct
    select, select_t = selections()
    params = pltpu.CompilerParams(vmem_limit_bytes=(64 << 20) - (64 << 10))
    smem = pltpu.SMEM
    vmem = pltpu.VMEM
    matrices = [vmem((LEAVES, RANK, PTS), F32), vmem((LEAVES - 1, RANK, 128), F32)]
    list_shape = (LISTS,)
    up, down, root = pl.pallas_call(
        up_kernel,
        out_shape=[
            shape((height, HALF), F32),
            shape((height, HALF), F32),
            shape((groups, vectors, 128), F32),
        ],
        in_specs=whole(4, pl.ANY),
        out_specs=whole(3, pl.ANY),
        scratch_shapes=[
            vmem((3, points), F32),
            vmem((groups, vectors, 128), F32),
            vmem((vectors, points), F32),
            vmem((ROWS, points), F32),
        ]
        + matrices
        + [vmem((vectors, 32 * 128), F32), pltpu.SemaphoreType.DMA((24,))],
        compiler_params=params,
    )(charges, coordinates, leaf_basis, local_transfer)

    upward = [(i, i + 1) for i in range(groups - 1)]
    lower = lax.ppermute(up, AXES, upward)
    upper = lax.ppermute(down, AXES, [(j, i) for i, j in upward])
    roots = lax.all_to_all(root, AXES, 0, 0)

    tile = vmem((PTS, PTS), BF16)
    tables = [
        vmem((LEAVES + 1, PTS, 32), BF16),
        vmem((LEAVES + 1, 2 * vectors, PTS), BF16),
    ]
    selects = [vmem(select.shape, BF16), vmem(select_t.shape, BF16)]
    near, targets, lists, entries = pl.pallas_call(
        near_kernel,
        out_shape=[
            shape((vectors, points), F32),
            shape((LEAVES, 32, PTS), BF16),
            shape(list_shape, jnp.int32),
            shape((SLOTS, 64), jnp.int32),
        ],
        in_specs=whole(6, pl.ANY),
        out_specs=whole(4, pl.ANY),
        scratch_shapes=[
            smem((SLOTS, LEAVES), jnp.int32),
            smem((SLOTS, NODES), jnp.int32),
            vmem((SLOTS, NODES), jnp.int32),
            smem(list_shape, jnp.int32),
            vmem((SLOTS, 64), jnp.int32),
            vmem((3, points), F32),
        ]
        + selects
        + [vmem((vectors, points), F32)] * 2
        + [vmem((LEAVES, 32, PTS), BF16)]
        + tables
        + [pltpu.SemaphoreType.DMA((16,))]
        + [tile] * (4 * LOCAL_GROUP),
        compiler_params=params,
        cost_estimate=pl.CostEstimate(
            flops=192 * 3 * 2 * PTS**3, transcendentals=192 * PTS**2, bytes_accessed=4 << 20
        ),
    )(near_lists.T, far_lists.T, charges, coordinates, select, select_t)

    skeletons = skeleton.transpose(1, 2, 0)
    return pl.pallas_call(
        functools.partial(down_kernel, groups),
        out_shape=shape((vectors, points), F32),
        in_specs=whole(15, pl.ANY),
        out_specs=pl.BlockSpec(memory_space=pl.ANY),
        scratch_shapes=[
            smem(list_shape, jnp.int32),
            smem((SLOTS, 64), jnp.int32),
            vmem((groups, vectors, 128), F32),
            vmem(skeletons.shape, F32),
            vmem(top_transfer.shape, F32),
            vmem(top_skeleton.shape, F32),
        ]
        + selects
        + [vmem((vectors, points), F32)] * 2
        + [vmem((LEAVES, 32, PTS), BF16)]
        + [vmem((height, HALF), F32)] * 3
        + matrices
        + tables
        + [
            vmem((2, 256, 128), F32),
            vmem((129 * 8, 128), F32),
            vmem((192, RANK, 128), BF16),
            vmem((QUADS, 128, 256), BF16),
            vmem((EMPTY + 1, 2 * vectors, 128), BF16),
            vmem((EMPTY + 1, 2 * vectors, 128), BF16),
            vmem((2 * QUADS + 2, vectors, 128), F32),
            vmem((groups, vectors, 128), F32),
            pltpu.SemaphoreType.DMA((24,)),
        ]
        + [tile] * (8 * GROUP),
        compiler_params=params,
    )(
        lists, entries, near, targets, lower, up, upper, leaf_basis, local_transfer,
        roots, skeletons, top_transfer, top_skeleton, select, select_t,
    )


def solution(mesh):
    placed = (
        P("vec", ("parts", "leaf", "sub")),
        P(None, ("parts", "leaf", "sub")),
        P(("parts", "leaf", "sub"), None),
        P(("parts", "leaf", "sub"), None),
        P(("parts", "leaf", "sub"), None, None),
        P(("parts", "leaf", "sub"), None, None),
        P("parts", None, None),
        P("parts", None, None),
        P("parts", None, None),
    )
    return jax.shard_map(
        on_device,
        mesh=mesh,
        in_specs=placed,
        out_specs=P("vec", ("parts", "leaf", "sub")),
        check_vma=False,
    )
```
